512 devices in a mesh: sess: 16 (over z), tile: 32 (over y, x, core).
Axes of the slice: x: 4, y: 4, z: 16, core: 2. Of those that a mesh axis runs over, the one named last changes fastest.
Arguments:
- features: bfloat16 [96, 64, 320, 128], P('sess', 'tile'), parts along dimension 0, may hold values from -6 to 6
- dec_weight: bfloat16 [9, 128, 128], replicated, may hold values from -0.1875 to 0.1875
- dec_bias: float32 [128], replicated, may hold values from -3 to 3
- first_weight: bfloat16 [9, 128, 128], replicated, may hold values from -0.1875 to 0.1875
- first_bias: float32 [128], replicated, may hold values from -3 to 3
- second_weight: bfloat16 [9, 128, 128], replicated, may hold values from -0.1875 to 0.1875
- second_bias: float32 [128], replicated, may hold values from -3 to 3
- boxes: int32 [3, 512], P(None, 'sess'), parts along dimension 1, may hold values from 0 to 336, as said below
- slots: int32 [1024], P('sess'), parts along dimension 0, may hold values from -1 to 31, as said below
Outputs:
- finished: bfloat16 [96, 64, 320, 128], P('sess', 'tile'), parts along dimension 0
- restorations: bfloat16 [1024, 64, 64, 128], P(('sess', 'tile')), parts along dimension 0
The draws below stay inside these ranges and needn't reach their ends.
There are 16 independent parts, one for each index of `sess`. The reference program is written for one: setup_inputs(seed, part) draws one part's arguments, and reference() takes and returns one part's arrays. A program takes and returns all parts, laid end to end along the dimension named above; an argument that names none is the same for every part. Nothing has to cross between parts.
Inputs may be any that keep to these rules, and one draw needn't show every extreme that they name: Column k of boxes is crop k: its first row r, its first column w and its size class c; the box has side 12 * (c + 2), and the square of side 48 at rows r, columns w lies inside the frame; some crop has class 3 - 1. `slots`: entries w * 2 to w * 2 + 1 are the crops that worker w restores, -1 marking an empty entry; each crop appears exactly once; some worker has 2 crops.
All inputs are finite; a program needn't handle non-finite values.
Results may differ from the reference program's by a relative error of at most 0.0057.
Values may be sent and summed in bfloat16 or wider, within the bound.
A program may use at most 64 MiB of HBM per device.

```python
import jax
import jax.numpy as jnp
from jax import lax

C = 128
S = 64
UNIT = 12
NCLS = 3
CAP = 2
BANDS = 6
COLS = 320
BAND_ROWS = 64
H = 384
CROPS = 32
SLOTS = 64


def draw_boxes(key, part):
    keys = jax.random.split(key, 4)
    span = UNIT * (NCLS + 1)
    row0 = jax.random.randint(keys[0], (CROPS,), 0, H - span + 1)
    col0 = jax.random.randint(keys[1], (CROPS,), 0, COLS - span + 1)
    size_class = jax.random.randint(keys[2], (CROPS,), 0, NCLS)
    chosen = jax.random.randint(keys[3], (), 0, CROPS)
    index = jnp.arange(CROPS)
    neighbour = (chosen + 1) % CROPS
    size_class = jnp.where(index == chosen, NCLS - 1, size_class)
    row0 = jnp.where(index == chosen, H - span, row0)
    col0 = jnp.where(index == chosen, 0, col0)
    col0 = jnp.where(index == neighbour, COLS - span, col0)
    return jnp.stack([row0, col0, size_class]).astype(jnp.int32)


def draw_slots(key, part):
    keys = jax.random.split(key, 2)
    workers = SLOTS // CAP
    owner = jax.random.randint(keys[0], (), 0, workers)
    index = jnp.arange(SLOTS, dtype=jnp.int32)
    score = jax.random.randint(keys[1], (SLOTS,), 0, 1 << 20) * SLOTS + index
    score = jnp.where(index // CAP == owner, -1 - index, score)
    order = jnp.argsort(score, stable=True)
    filled = jnp.full((SLOTS,), -1, jnp.int32)
    return filled.at[order[:CROPS]].set(jnp.arange(CROPS, dtype=jnp.int32))


def block_levels(rng, dims, cuts, low, high):
    loudness = 1.0
    for axis_at, shards_of in cuts:
        steps = jax.random.uniform(jax.random.fold_in(jax.random.fold_in(rng, 6), axis_at), (shards_of,), jnp.float32, low / len(cuts), high / len(cuts))
        loudness = loudness * jnp.repeat(jnp.exp(steps), dims[axis_at] // shards_of).reshape((-1,) + (1,) * (len(dims) - 1 - axis_at))
    return loudness


def gaussian(rng, extent, deviation, most, shards=(), kind=jnp.bfloat16):
    result = jax.random.normal(rng, extent, jnp.float32) * deviation
    if len(shards) > 0:
        result = block_levels(rng, extent, shards, -0.22, 0.18) * result
    return jnp.clip(result, min=-most, max=most).astype(kind)


def setup_inputs(seed: int = 0, part: int = 0) -> dict:
    key_of = jax.random.split(jax.random.key(seed), 10)
    part_keys = jax.random.split(jax.random.fold_in(key_of[9], part), 10)
    return {
        "features": gaussian(part_keys[0], (BANDS, BAND_ROWS, COLS, C), 1.0, 6.0, ((1, 32),)),
        "dec_weight": gaussian(key_of[1], (9, C, C), (9 * C) ** -0.5, 0.1875),
        "dec_bias": gaussian(key_of[2], (C,), 0.5, 3.0, (), jnp.float32),
        "first_weight": gaussian(key_of[3], (9, C, C), (9 * C) ** -0.5, 0.1875),
        "first_bias": gaussian(key_of[4], (C,), 0.5, 3.0, (), jnp.float32),
        "second_weight": gaussian(key_of[5], (9, C, C), (9 * C) ** -0.5, 0.1875),
        "second_bias": gaussian(key_of[6], (C,), 0.5, 3.0, (), jnp.float32),
        "boxes": draw_boxes(jax.random.fold_in(jax.random.fold_in(key_of[9], part), 71), part),
        "slots": draw_slots(jax.random.fold_in(jax.random.fold_in(key_of[9], part), 71), part),
    }


def hat_down(length, cells, size_out):
    lenf = length.astype(jnp.float32)
    spots = (jnp.arange(size_out, dtype=jnp.float32) + 0.5) * lenf / size_out - 0.5
    spots = jnp.clip(spots, 0.0, lenf - 1.0)
    return jnp.maximum(0.0, 1.0 - jnp.abs(spots[:, None] - cells[None, :]))


def hat_up(length, cells, size_in):
    lenf = length.astype(jnp.float32)
    spots = (cells + 0.5) * size_in / lenf - 0.5
    spots = jnp.clip(spots, 0.0, size_in - 1.0)
    inside = ((cells >= 0.0) & (cells < lenf)).astype(jnp.float32)
    grid = jnp.arange(size_in, dtype=jnp.float32)
    return jnp.maximum(0.0, 1.0 - jnp.abs(spots[:, None] - grid[None, :])) * inside[:, None]


def conv_ref(padded, weight):
    height = padded.shape[-3] - 2
    width = padded.shape[-2] - 2
    total = None
    for tap in range(9):
        down, right = tap // 3, tap % 3
        part = padded[..., down:down + height, right:right + width, :]
        term = jnp.einsum('...hwk,kd->...hwd', part.astype(jnp.float32), weight[tap].astype(jnp.float32))
        total = term if total is None else total + term
    return total


def restore_ref(crops, first_weight, first_bias, second_weight, second_bias):
    padded = jnp.pad(crops, ((0, 0), (1, 1), (1, 1), (0, 0)))
    inner = jax.nn.silu(conv_ref(padded, first_weight) + first_bias).astype(jnp.bfloat16)
    padded = jnp.pad(inner, ((0, 0), (1, 1), (1, 1), (0, 0)))
    return (conv_ref(padded, second_weight) + second_bias).astype(jnp.bfloat16)


def reference(features, dec_weight, dec_bias, first_weight, first_bias, second_weight, second_bias, boxes, slots):
    span = UNIT * (NCLS + 1)
    bands, band_rows, cols, chans = features.shape
    height = bands * band_rows
    frame = features.reshape(height, cols, chans)
    padded = jnp.pad(frame, ((1, 1), (1, 1), (0, 0)))
    decoded = (frame.astype(jnp.float32) + jax.nn.silu(conv_ref(padded, dec_weight) + dec_bias)).astype(jnp.bfloat16)
    cells = jnp.arange(span, dtype=jnp.float32)
    highest = lax.Precision.HIGHEST
    anchor = jnp.zeros((), jnp.int32)

    def cut(index):
        row0 = boxes[0, index].astype(jnp.int32)
        col0 = boxes[1, index].astype(jnp.int32)
        length = UNIT * (boxes[2, index] + 2)
        region = lax.dynamic_slice(decoded, (row0, col0, anchor), (span, span, chans))
        across = hat_down(length, cells, S)
        colcut = jnp.einsum('tw,hwc->htc', across, region.astype(jnp.float32), precision=highest).astype(jnp.bfloat16)
        return jnp.einsum('sh,htc->stc', across, colcut.astype(jnp.float32), precision=highest).astype(jnp.bfloat16)

    crops = lax.map(cut, jnp.arange(CROPS, dtype=jnp.int32))
    deltas = restore_ref(crops, first_weight, first_bias, second_weight, second_bias)
    picked = deltas[jnp.maximum(slots, 0)]
    restorations = jnp.where((slots >= 0)[:, None, None, None], picked, jnp.zeros_like(picked))

    def paste(index, canvas):
        row0 = boxes[0, index].astype(jnp.int32)
        col0 = boxes[1, index].astype(jnp.int32)
        length = UNIT * (boxes[2, index] + 2)
        lift = hat_up(length, cells, S)
        upper = jnp.einsum('hs,stc->htc', lift, deltas[index].astype(jnp.float32), precision=highest).astype(jnp.bfloat16)
        patch = jnp.einsum('wt,htc->hwc', lift, upper.astype(jnp.float32), precision=highest).astype(jnp.bfloat16)
        old = lax.dynamic_slice(canvas, (row0, col0, anchor), (span, span, chans))
        return lax.dynamic_update_slice(canvas, old + patch.astype(jnp.float32), (row0, col0, anchor))

    canvas = lax.fori_loop(0, CROPS, paste, jnp.zeros((height + span, cols + span, chans), jnp.float32))
    finished = (decoded.astype(jnp.float32) + canvas[:height, :cols]).astype(jnp.bfloat16)
    return (finished.reshape(bands, band_rows, cols, chans), restorations)
```

```python
import functools

import jax
import jax.numpy as jnp
from jax import lax
from jax.experimental import pallas as pl
from jax.experimental.pallas import tpu as pltpu
from jax.sharding import PartitionSpec as P

S = 64
UNIT = 12
SPAN = 48
C = 128
BANDS = 6
COLS = 320
STRIDE = 64
TILES = 32
CAP = 2
MESH = pl.DeviceIdType.MESH
BF = jnp.bfloat16
F32 = jnp.float32

OFFSETS = sorted(
    [(dy, dx, dc) for dy in range(4) for dx in range(4) for dc in range(2) if dy + dx + dc],
    key=lambda d: -(min(d[0], 4 - d[0]) + min(d[1], 4 - d[1])),
)


def silu(v):
    return v * (1.0 / (1.0 + jnp.exp(-v)))


def rounded(v):
    return v.astype(BF).astype(F32)


def pair_weight(w_ref, out_ref):
    zero = jnp.zeros((C, C), BF)
    for a in range(4):
        for dx in range(3):
            rows = pl.ds((a * 3 + dx) * C, C)
            out_ref[rows, 0:C] = w_ref[3 * a + dx] if a < 3 else zero
            out_ref[rows, C : 2 * C] = w_ref[3 * (a - 1) + dx] if a > 0 else zero


def widen(pad_ref, index, cols):
    return jnp.concatenate(
        [pad_ref[index, pl.ds(7 + dx, cols), :].astype(BF) for dx in range(3)], axis=-1
    )


def side_of(boxes, crop):
    return UNIT * (boxes[2, crop] + 2)


def decode_kernel(
    boxes, slots, feat, above, below, w_ref, b_ref, dec, payload, w_pair, pad, wide, held
):
    position = lax.axis_index("tile")
    pair_weight(w_ref, w_pair)
    pad[:, 0:8, :] = jnp.zeros((4, 8, C), F32)
    pad[:, COLS + 8 : COLS + 16, :] = jnp.zeros((4, 8, C), F32)
    bias = jnp.concatenate([b_ref[...], b_ref[...]], axis=-1)

    def band(b, _):
        up = jnp.where(position == 0, b - 1, b)
        down = jnp.where(position == TILES - 1, b + 1, b)
        up_ok = (up >= 0).astype(F32)
        down_ok = (down < BANDS).astype(F32)
        pad[0, 8 : COLS + 8, :] = above[jnp.maximum(up, 0)].astype(F32) * up_ok
        pad[1, 8 : COLS + 8, :] = feat[b, 0].astype(F32)
        pad[2, 8 : COLS + 8, :] = feat[b, 1].astype(F32)
        pad[3, 8 : COLS + 8, :] = below[jnp.minimum(down, BANDS - 1)].astype(F32) * down_ok
        for a in range(4):
            wide[a] = widen(pad, a, COLS)
        for part in range(2):
            rows = pl.ds(part * (COLS // 2), COLS // 2)
            lhs = jnp.concatenate([wide[a, rows, :] for a in range(4)], axis=-1)
            acc = jnp.dot(lhs, w_pair[...], preferred_element_type=F32) + bias
            act = silu(acc)
            for o in range(2):
                v = (feat[b, o, rows, :].astype(F32) + act[:, o * C : (o + 1) * C]).astype(BF)
                dec[b, o, rows, :] = v
                held[2 * b + o, rows, :] = v.astype(F32)
        return 0

    lax.fori_loop(0, BANDS, band, 0)

    def fill(q, _):
        crop = jnp.maximum(slots[q], 0)
        row0 = boxes[0, crop]
        col0 = boxes[1, crop]
        for i in range(2):
            h = (2 * position + i - row0) & (STRIDE - 1)
            row = 2 * jnp.minimum((row0 + h) >> 6, BANDS - 1) + i
            payload[q, i] = held[row, pl.ds(col0, SPAN), :].astype(BF)
        return 0

    lax.fori_loop(0, TILES * CAP, fill, 0, unroll=2)


def exchange_kernel(src, dst, send_sem, recv_sem, own_sem):
    me = lax.axis_index("tile")
    y, x, core = me // 8, (me // 2) % 4, me % 2
    targets = [
        ((y + dy) % 4) * 8 + ((x + dx) % 4) * 2 + (core + dc) % 2 for dy, dx, dc in OFFSETS
    ]
    barrier = pltpu.get_barrier_semaphore()
    for t in targets:
        pl.semaphore_signal(barrier, inc=1, device_id={"tile": t}, device_id_type=MESH)
    own = pltpu.make_async_copy(src.at[me], dst.at[me], own_sem)
    own.start()
    pl.semaphore_wait(barrier, TILES - 1)
    copies = [
        pltpu.make_async_remote_copy(
            src_ref=src.at[t],
            dst_ref=dst.at[me],
            send_sem=send_sem.at[k],
            recv_sem=recv_sem.at[k],
            device_id={"tile": t},
            device_id_type=MESH,
        )
        for k, t in enumerate(targets)
    ]
    for copy in copies:
        copy.start()
    own.wait()
    for copy in copies:
        copy.wait()


def exchange(x, collective_id):
    n = len(OFFSETS)
    return pl.pallas_call(
        exchange_kernel,
        out_shape=jax.ShapeDtypeStruct(x.shape, x.dtype),
        in_specs=[pl.BlockSpec(memory_space=pl.ANY)],
        out_specs=pl.BlockSpec(memory_space=pl.ANY),
        scratch_shapes=[
            pltpu.SemaphoreType.DMA((n,)),
            pltpu.SemaphoreType.DMA((n,)),
            pltpu.SemaphoreType.DMA,
        ],
        compiler_params=pltpu.CompilerParams(collective_id=collective_id, has_side_effects=True),
        name=f"exchange_{collective_id}",
    )(x)


CHUNK = 4


def conv_pairs(wide, w_pair, bias, m0):
    lhs = jnp.concatenate(
        [
            wide[pl.ds(m0 + a // 2, CHUNK), a % 2].reshape(CHUNK * S, 3 * C)
            for a in range(4)
        ],
        axis=-1,
    )
    return jnp.dot(lhs, w_pair[...], preferred_element_type=F32) + bias


def restore_kernel(
    boxes, slots, got, w1, b1, w2, b2, rest, back, w1_pair, w2_pair, cut, pad, wide, wide2, delta
):
    step = pl.program_id(0)
    position = lax.axis_index("tile")

    @pl.when(step == 0)
    def _():
        pair_weight(w1, w1_pair)
        pair_weight(w2, w2_pair)
        pad[:, 0:8, :] = jnp.zeros((S, 8, C), F32)
        pad[:, S + 8 : S + 16, :] = jnp.zeros((S, 8, C), F32)
        for ref in (wide, wide2):
            ref[0, 0] = jnp.zeros((S, 3 * C), BF)
            ref[S // 2, 1] = jnp.zeros((S, 3 * C), BF)

    slot = slots[CAP * position + step]
    crop = jnp.maximum(slot, 0)
    row0 = boxes[0, crop]
    side = side_of(boxes, crop)
    sidef = side.astype(F32)

    spot = (lax.broadcasted_iota(jnp.int32, (S, SPAN), 0).astype(F32) + 0.5) * sidef / S - 0.5
    spot = jnp.clip(spot, 0.0, sidef - 1.0)
    cell = lax.broadcasted_iota(jnp.int32, (S, SPAN), 1).astype(F32)
    down = jnp.maximum(0.0, 1.0 - jnp.abs(spot - cell)).astype(BF)

    def colcut(p, _):
        rhs = jnp.concatenate([got[p, 0, 0], got[p, 0, 1]], axis=-1)
        y = rounded(jnp.dot(down, rhs, preferred_element_type=F32))
        cut[2 * p] = y[:, 0:C]
        cut[2 * p + 1] = y[:, C : 2 * C]
        return 0

    lax.fori_loop(0, TILES, colcut, 0, unroll=4)

    def crop_row(s, _):
        num = jnp.clip((2 * s + 1) * side - S, 0, (side - 1) * 128)
        first = num >> 7
        second = jnp.minimum(first + 1, SPAN - 1)
        frac = (num & 127).astype(F32) * (1.0 / 128.0)
        a = cut[(row0 + first) & (STRIDE - 1)]
        b = cut[(row0 + second) & (STRIDE - 1)]
        pad[s, 8 : S + 8, :] = rounded((1.0 - frac) * a + frac * b)
        return 0

    lax.fori_loop(0, S, crop_row, 0, unroll=4)

    def spread(target):
        def body(s, _):
            target[(s + 1) >> 1, (s + 1) & 1] = widen(pad, s, S)
            return 0

        lax.fori_loop(0, S, body, 0, unroll=4)

    spread(wide)
    bias1 = jnp.concatenate([b1[...], b1[...]], axis=-1)
    bias2 = jnp.concatenate([b2[...], b2[...]], axis=-1)

    def first(j, _):
        v = rounded(silu(conv_pairs(wide, w1_pair, bias1, j * CHUNK)))
        v = v.reshape(CHUNK, S, 2 * C)
        for i in range(CHUNK):
            for o in range(2):
                pad[2 * (j * CHUNK + i) + o, 8 : S + 8, :] = v[i, :, o * C : (o + 1) * C]
        return 0

    lax.fori_loop(0, S // 2 // CHUNK, first, 0)
    spread(wide2)
    keep = slot >= 0

    def second(j, _):
        v = rounded(conv_pairs(wide2, w2_pair, bias2, j * CHUNK))
        v = v.reshape(CHUNK, S, 2 * C)
        for i in range(CHUNK):
            for o in range(2):
                row = 2 * (j * CHUNK + i) + o
                part = v[i, :, o * C : (o + 1) * C]
                delta[row] = part
                rest[0, row] = jnp.where(keep, part, 0.0).astype(BF)
        return 0

    lax.fori_loop(0, S // 2 // CHUNK, second, 0)

    where = (lax.broadcasted_iota(jnp.int32, (SPAN, S), 0).astype(F32) + 0.5) * S / sidef - 0.5
    where = jnp.clip(where, 0.0, S - 1.0)
    inside = lax.broadcasted_iota(jnp.int32, (SPAN, S), 0) < side
    grid = lax.broadcasted_iota(jnp.int32, (SPAN, S), 1).astype(F32)
    lift = jnp.where(inside, jnp.maximum(0.0, 1.0 - jnp.abs(where - grid)), 0.0)
    lift_high = lift.astype(BF)
    lift_low = (lift - lift_high.astype(F32)).astype(BF)
    lifts = jnp.concatenate([lift_high, lift_low], axis=-1)
    magic = jnp.where(side == 24, 10923, jnp.where(side == 36, 7282, 5462))

    def patch(p, _):
        halves = []
        for i in range(2):
            h = (2 * p + i - row0) & (STRIDE - 1)
            num = jnp.clip((2 * h + 1) * (S // 2) - (side >> 1), 0, (S - 1) * side)
            one = (num * magic) >> 18
            frac = (num - one * side).astype(F32) / sidef
            live = (h < side).astype(F32)
            two = jnp.minimum(one + 1, S - 1)
            halves.append(
                ((live * (1.0 - frac)) * delta[one] + (live * frac) * delta[two]).astype(BF)
            )
        rhs = jnp.concatenate(halves, axis=-1)
        rhs = jnp.concatenate([rhs, rhs], axis=0)
        y = jnp.dot(lifts, rhs, preferred_element_type=F32).astype(BF)
        back[p, 0, 0] = y[:, 0:C]
        back[p, 0, 1] = y[:, C : 2 * C]
        return 0

    lax.fori_loop(0, TILES, patch, 0, unroll=4)


def paste_kernel(boxes, slots, dec, back, out, acc):
    position = lax.axis_index("tile")
    for b in range(BANDS):
        for o in range(2):
            acc[2 * b + o] = dec[b, o].astype(F32)

    def body(q, _):
        slot = slots[q]
        crop = jnp.maximum(slot, 0)
        row0 = boxes[0, crop]
        cols = pl.ds(boxes[1, crop], SPAN)
        for i in range(2):
            h = (2 * position + i - row0) & (STRIDE - 1)
            live = (slot >= 0) & (h < SPAN)
            row = jnp.where(live, 2 * ((row0 + h) >> 6) + i, 2 * BANDS + i)
            acc[row, cols, :] = acc[row, cols, :] + back[q, i].astype(F32)
        return 0

    lax.fori_loop(0, TILES * CAP, body, 0, unroll=2)
    for b in range(BANDS):
        for o in range(2):
            out[b, o] = acc[2 * b + o].astype(BF)


def shards(
    features,
    dec_weight,
    dec_bias,
    first_weight,
    first_bias,
    second_weight,
    second_bias,
    boxes,
    slots,
):
    ring = [(i, (i + 1) % TILES) for i in range(TILES)]
    above = lax.ppermute(features[:, 1], "tile", ring)
    below = lax.ppermute(features[:, 0], "tile", [(j, i) for i, j in ring])
    smem = pl.BlockSpec(memory_space=pltpu.SMEM)
    vmem = pl.BlockSpec(memory_space=pltpu.VMEM)
    limit = 60 * 1024 * 1024
    rows = (TILES * CAP, 2, SPAN, C)

    decoded, payload = pl.pallas_call(
        decode_kernel,
        out_shape=(
            jax.ShapeDtypeStruct(features.shape, BF),
            jax.ShapeDtypeStruct(rows, BF),
        ),
        in_specs=[smem, smem] + [vmem] * 5,
        out_specs=(vmem, vmem),
        scratch_shapes=[
            pltpu.VMEM((12 * C, 2 * C), BF),
            pltpu.VMEM((4, COLS + 16, C), F32),
            pltpu.VMEM((4, COLS, 3 * C), BF),
            pltpu.VMEM((2 * BANDS, COLS, C), F32),
        ],
        compiler_params=pltpu.CompilerParams(vmem_limit_bytes=limit),
        name="decode",
    )(boxes, slots, features, above, below, dec_weight, dec_bias[None])

    blocks = (TILES, CAP, 2, SPAN, C)
    got = exchange(payload.reshape(blocks), 0)

    const = lambda shape: pl.BlockSpec(shape, lambda s: (0,) * len(shape))
    rest, back = pl.pallas_call(
        restore_kernel,
        grid=(CAP,),
        out_shape=(
            jax.ShapeDtypeStruct((CAP, S, S, C), BF),
            jax.ShapeDtypeStruct(blocks, BF),
        ),
        in_specs=[
            smem,
            smem,
            pl.BlockSpec((TILES, 1, 2, SPAN, C), lambda s: (0, s, 0, 0, 0)),
            const((9, C, C)),
            const((1, C)),
            const((9, C, C)),
            const((1, C)),
        ],
        out_specs=(
            pl.BlockSpec((1, S, S, C), lambda s: (s, 0, 0, 0)),
            pl.BlockSpec((TILES, 1, 2, SPAN, C), lambda s: (0, s, 0, 0, 0)),
        ),
        scratch_shapes=[
            pltpu.VMEM((12 * C, 2 * C), BF),
            pltpu.VMEM((12 * C, 2 * C), BF),
            pltpu.VMEM((S, S, C), F32),
            pltpu.VMEM((S, S + 16, C), F32),
            pltpu.VMEM((S // 2 + 1, 2, S, 3 * C), BF),
            pltpu.VMEM((S // 2 + 1, 2, S, 3 * C), BF),
            pltpu.VMEM((S, S, C), F32),
        ],
        compiler_params=pltpu.CompilerParams(vmem_limit_bytes=limit),
        name="restore",
    )(boxes, slots, got, first_weight, first_bias[None], second_weight, second_bias[None])

    returned = exchange(back, 1)
    finished = pl.pallas_call(
        paste_kernel,
        out_shape=jax.ShapeDtypeStruct(features.shape, BF),
        in_specs=[smem, smem, vmem, vmem],
        out_specs=vmem,
        scratch_shapes=[pltpu.VMEM((2 * BANDS + 2, COLS, C), F32)],
        compiler_params=pltpu.CompilerParams(vmem_limit_bytes=limit),
        name="paste",
    )(boxes, slots, decoded, returned.reshape(rows))
    return finished, rest


def solution(mesh):
    return jax.shard_map(
        shards,
        mesh=mesh,
        in_specs=(
            P("sess", "tile", None, None),
            P(),
            P(),
            P(),
            P(),
            P(),
            P(),
            P(None, "sess"),
            P("sess"),
        ),
        out_specs=(P("sess", "tile", None, None), P(("sess", "tile"), None, None, None)),
        check_vma=False,
    )
```

```python
import jax
import jax.numpy as jnp
from jax import lax
from jax.experimental import pallas as pl
from jax.experimental.pallas import tpu as pltpu
from jax.sharding import PartitionSpec as P

S = 64
UNIT = 12
SPAN = 48
C = 128
BANDS = 6
COLS = 320
STRIDE = 64
TILES = 32
CAP = 2
FRAME = BANDS * STRIDE
SENT = 56
MESH = pl.DeviceIdType.MESH
BF = jnp.bfloat16
F32 = jnp.float32
CHUNK = 4
VMEM_LIMIT = 60 * 1024 * 1024

OFFSETS = sorted(
    [(dy, dx, dc) for dy in range(4) for dx in range(4) for dc in range(2) if dy + dx + dc],
    key=lambda d: -(min(d[0], 4 - d[0]) + min(d[1], 4 - d[1])),
)
PEERS = len(OFFSETS)


def silu(v):
    return v * (1.0 / (1.0 + jnp.exp(-v)))


def rounded(v):
    return v.astype(BF).astype(F32)


def pair_weight(w_ref, out_ref):
    zero = jnp.zeros((C, C), BF)
    for a in range(4):
        for dx in range(3):
            rows = pl.ds((a * 3 + dx) * C, C)
            out_ref[rows, 0:C] = w_ref[3 * a + dx] if a < 3 else zero
            out_ref[rows, C : 2 * C] = w_ref[3 * (a - 1) + dx] if a > 0 else zero


def widen(pad_ref, index, start, cols):
    return jnp.concatenate(
        [pad_ref[index, pl.ds(start + dx, cols), :].astype(BF) for dx in range(3)], axis=-1
    )


def conv_pairs(wide, w_pair, bias, m0, cols):
    lhs = jnp.concatenate(
        [
            wide[pl.ds(m0 + a // 2, CHUNK), a % 2].reshape(CHUNK * cols, 3 * C)
            for a in range(4)
        ],
        axis=-1,
    )
    return jnp.dot(lhs, w_pair[...], preferred_element_type=F32) + bias


def twice(b_ref):
    return jnp.concatenate([b_ref[...], b_ref[...]], axis=-1)


def main_kernel(
    boxes,
    slots,
    feat,
    w0,
    b0,
    w1,
    b1,
    w2,
    b2,
    dec_out,
    rest_out,
    back,
    w0_pair,
    w1_pair,
    w2_pair,
    fpad,
    payload,
    got,
    reg,
    wide0,
    cut,
    pad,
    pad2,
    wide,
    wide2,
    delta,
    rest,
    ret,
    halo,
    hpad,
    dwide,
    dec,
    fwd_send,
    fwd_recv,
    ret_send,
    ret_recv,
    halo_send,
    halo_recv,
    local_sem,
):
    me = lax.axis_index("tile")
    y, x, core = me // 8, (me // 2) % 4, me % 2
    targets = [
        ((y + dy) % 4) * 8 + ((x + dx) % 4) * 2 + (core + dc) % 2 for dy, dx, dc in OFFSETS
    ]
    barrier = pltpu.get_barrier_semaphore()
    for t in targets:
        pl.semaphore_signal(barrier, inc=1, device_id={"tile": t}, device_id_type=MESH)

    def remote(src, dst, send, recv, t):
        return pltpu.make_async_remote_copy(
            src_ref=src,
            dst_ref=dst,
            send_sem=send,
            recv_sem=recv,
            device_id={"tile": t},
            device_id_type=MESH,
        )

    def forward(s):
        return [
            remote(
                payload.at[s, t], got.at[s, me], fwd_send.at[s, k], fwd_recv.at[s, k], t
            )
            for k, t in enumerate(targets)
        ]

    def backward(s):
        return [
            remote(ret.at[s, t], back.at[s, me], ret_send.at[s, k], ret_recv.at[s, k], t)
            for k, t in enumerate(targets)
        ]

    def own_forward(s):
        return pltpu.make_async_copy(payload.at[s, me], got.at[s, me], local_sem.at[s])

    def own_backward(s):
        return pltpu.make_async_copy(ret.at[s, me], back.at[s, me], local_sem.at[2 + s])

    def keep_rest(s):
        return pltpu.make_async_copy(rest.at[s], rest_out.at[s], local_sem.at[4 + s])

    def rims():
        after, ahead = (me + 1) % TILES, (me + TILES - 1) % TILES
        return [
            remote(feat.at[:, 1], halo.at[0], halo_send.at[0], halo_recv.at[0], after),
            remote(feat.at[:, 0], halo.at[1], halo_send.at[1], halo_recv.at[1], ahead),
        ]

    fpad[:, 0:8, :] = jnp.zeros((2 * BANDS, 8, C), F32)
    fpad[:, COLS + 8 : COLS + 16, :] = jnp.zeros((2 * BANDS, 8, C), F32)
    for b in range(BANDS):
        for o in range(2):
            fpad[2 * b + o, 8 : COLS + 8, :] = feat[b, o].astype(F32)

    def fill(s):
        def body(w, _):
            crop = jnp.maximum(slots[CAP * w + s], 0)
            row0 = boxes[0, crop] - 1
            col0 = boxes[1, crop]
            parts = []
            for i in range(2):
                h = (2 * me + i - row0) & (STRIDE - 1)
                band = jnp.clip((row0 + h) >> 6, 0, BANDS - 1)
                parts.append(fpad[2 * band + i, pl.ds(col0 + 7, SENT), :])
            payload[s, w] = jnp.concatenate(parts, axis=0).astype(BF)
            return 0

        lax.fori_loop(0, TILES, body, 0, unroll=2)

    fill(0)
    pl.semaphore_wait(barrier, PEERS)
    for copy in forward(0):
        copy.start()
    own_forward(0).start()
    fill(1)
    for copy in forward(1):
        copy.start()
    own_forward(1).start()
    for copy in rims():
        copy.start()

    pair_weight(w0, w0_pair)
    pair_weight(w1, w1_pair)
    pair_weight(w2, w2_pair)
    for ref in (pad, pad2):
        ref[:, 0:8, :] = jnp.zeros((S, 8, C), F32)
        ref[:, S + 8 : S + 16, :] = jnp.zeros((S, 8, C), F32)
    for ref in (wide, wide2):
        ref[0, 0] = jnp.zeros((S, 3 * C), BF)
        ref[S // 2, 1] = jnp.zeros((S, 3 * C), BF)
    reg[STRIDE] = jnp.zeros((SENT, C), F32)
    hpad[:, 0:8, :] = jnp.zeros((2, 8, C), F32)
    hpad[:, COLS + 8 : COLS + 16, :] = jnp.zeros((2, 8, C), F32)
    bias0, bias1, bias2 = twice(b0), twice(b1), twice(b2)

    def restore(s, _):
        own_forward(s).wait()
        for copy in forward(s):
            copy.wait_recv()
        slot = slots[CAP * me + s]
        crop = jnp.maximum(slot, 0)
        row0 = boxes[0, crop]
        side = UNIT * (boxes[2, crop] + 2)
        sidef = side.astype(F32)

        def unpack(p, _):
            block = got[s, p].astype(F32)
            reg[2 * p] = block[0:SENT]
            reg[2 * p + 1] = block[SENT : 2 * SENT]
            return 0

        lax.fori_loop(0, TILES, unpack, 0, unroll=4)

        def region(h, _):
            for o in range(2):
                row = row0 - 1 + 2 * h + o
                live = (row >= 0) & (row < FRAME)
                index = jnp.where(live, row & (STRIDE - 1), STRIDE)
                wide0[h, o] = widen(reg, index, 0, SPAN)
            return 0

        lax.fori_loop(0, SPAN // 2 + 1, region, 0)

        spot = (lax.broadcasted_iota(jnp.int32, (S, SPAN), 0).astype(F32) + 0.5) * sidef / S
        spot = jnp.clip(spot - 0.5, 0.0, sidef - 1.0)
        cell = lax.broadcasted_iota(jnp.int32, (S, SPAN), 1).astype(F32)
        down = jnp.maximum(0.0, 1.0 - jnp.abs(spot - cell)).astype(BF)

        def decode(j, _):
            m0 = j * CHUNK
            act = silu(conv_pairs(wide0, w0_pair, bias0, m0, SPAN))
            act = act.reshape(CHUNK, SPAN, 2 * C)
            for i in range(CHUNK):
                centre = jnp.concatenate(
                    [wide0[m0 + i, 1, :, C : 2 * C], wide0[m0 + i + 1, 0, :, C : 2 * C]], axis=-1
                )
                value = (centre.astype(F32) + act[i]).astype(BF)
                z = rounded(jnp.dot(down, value, preferred_element_type=F32))
                cut[2 * (m0 + i)] = z[:, 0:C]
                cut[2 * (m0 + i) + 1] = z[:, C : 2 * C]
            return 0

        lax.fori_loop(0, SPAN // 2 // CHUNK, decode, 0)

        def spread(source, target, group):
            for k in range(2 * CHUNK):
                row = group * 2 * CHUNK + k
                target[(row + 1) >> 1, (row + 1) & 1] = widen(source, row, 7, S)

        def crop_rows(g, _):
            spread(pad, wide, jnp.maximum(g - 1, 0))
            for k in range(2 * CHUNK):
                t = g * 2 * CHUNK + k
                num = jnp.clip((2 * t + 1) * side - S, 0, (side - 1) * 128)
                first = num >> 7
                second = jnp.minimum(first + 1, SPAN - 1)
                frac = (num & 127).astype(F32) * (1.0 / 128.0)
                pad[t, 8 : S + 8, :] = rounded((1.0 - frac) * cut[first] + frac * cut[second])
            return 0

        groups = S // (2 * CHUNK)
        lax.fori_loop(0, groups, crop_rows, 0)
        spread(pad, wide, groups - 1)

        def first_conv(j, _):
            spread(pad2, wide2, jnp.maximum(j - 1, 0))
            v = rounded(silu(conv_pairs(wide, w1_pair, bias1, j * CHUNK, S)))
            v = v.reshape(CHUNK, S, 2 * C)
            for i in range(CHUNK):
                for o in range(2):
                    pad2[2 * (j * CHUNK + i) + o, 8 : S + 8, :] = v[i, :, o * C : (o + 1) * C]
            return 0

        lax.fori_loop(0, groups, first_conv, 0)
        spread(pad2, wide2, groups - 1)
        keep = slot >= 0

        def second_conv(j, _):
            v = rounded(conv_pairs(wide2, w2_pair, bias2, j * CHUNK, S))
            v = v.reshape(CHUNK, S, 2 * C)
            for i in range(CHUNK):
                for o in range(2):
                    row = 2 * (j * CHUNK + i) + o
                    part = v[i, :, o * C : (o + 1) * C]
                    delta[row] = part
                    rest[s, row] = jnp.where(keep, part, 0.0).astype(BF)
            return 0

        lax.fori_loop(0, groups, second_conv, 0)
        keep_rest(s).start()

        where = (lax.broadcasted_iota(jnp.int32, (SPAN, S), 0).astype(F32) + 0.5) * S / sidef
        where = jnp.clip(where - 0.5, 0.0, S - 1.0)
        inside = lax.broadcasted_iota(jnp.int32, (SPAN, S), 0) < side
        grid = lax.broadcasted_iota(jnp.int32, (SPAN, S), 1).astype(F32)
        lift = jnp.where(inside, jnp.maximum(0.0, 1.0 - jnp.abs(where - grid)), 0.0)
        lift_high = lift.astype(BF)
        lift_low = (lift - lift_high.astype(F32)).astype(BF)
        lifts = jnp.concatenate([lift_high, lift_low], axis=-1)
        magic = jnp.where(side == 24, 10923, jnp.where(side == 36, 7282, 5462))
        inverse = jnp.where(side == 24, 1.0 / 24, jnp.where(side == 36, 1.0 / 36, 1.0 / 48))

        def patch(p, _):
            halves = []
            for i in range(2):
                h = (2 * p + i - row0) & (STRIDE - 1)
                num = jnp.clip((2 * h + 1) * (S // 2) - (side >> 1), 0, (S - 1) * side)
                one = (num * magic) >> 18
                frac = (num - one * side).astype(F32) * inverse
                live = (h < side).astype(F32)
                two = jnp.minimum(one + 1, S - 1)
                halves.append(
                    ((live - live * frac) * delta[one] + (live * frac) * delta[two]).astype(BF)
                )
            rhs = jnp.concatenate(halves, axis=-1)
            rhs = jnp.concatenate([rhs, rhs], axis=0)
            z = jnp.dot(lifts, rhs, preferred_element_type=F32).astype(BF)
            ret[s, p, 0] = z[:, 0:C]
            ret[s, p, 1] = z[:, C : 2 * C]
            return 0

        lax.fori_loop(0, TILES, patch, 0, unroll=4)
        for copy in backward(s):
            copy.start()
        own_backward(s).start()
        return 0

    lax.fori_loop(0, CAP, restore, 0)

    for copy in rims():
        copy.wait_recv()

    def band(b, _):
        up = jnp.where(me == 0, b - 1, b)
        low = jnp.where(me == TILES - 1, b + 1, b)
        up_ok = (up >= 0).astype(F32)
        low_ok = (low < BANDS).astype(F32)
        hpad[0, 8 : COLS + 8, :] = halo[0, jnp.maximum(up, 0)].astype(F32) * up_ok
        hpad[1, 8 : COLS + 8, :] = halo[1, jnp.minimum(low, BANDS - 1)].astype(F32) * low_ok
        dwide[0] = widen(hpad, 0, 7, COLS)
        dwide[1] = widen(fpad, 2 * b, 7, COLS)
        dwide[2] = widen(fpad, 2 * b + 1, 7, COLS)
        dwide[3] = widen(hpad, 1, 7, COLS)
        for part in range(2):
            rows = pl.ds(part * (COLS // 2), COLS // 2)
            lhs = jnp.concatenate([dwide[a, rows, :] for a in range(4)], axis=-1)
            act = silu(jnp.dot(lhs, w0_pair[...], preferred_element_type=F32) + bias0)
            for o in range(2):
                v = feat[b, o, rows, :].astype(F32) + act[:, o * C : (o + 1) * C]
                dec[b, o, rows, :] = v.astype(BF)
        return 0

    lax.fori_loop(0, BANDS, band, 0)
    out = pltpu.make_async_copy(dec, dec_out, local_sem.at[6])
    out.start()
    for copy in rims():
        copy.wait_send()
    for s in range(CAP):
        for copy in forward(s):
            copy.wait_send()
        keep_rest(s).wait()
        own_backward(s).wait()
    for s in range(CAP):
        for copy in backward(s):
            copy.wait()
    out.wait()


def paste_kernel(boxes, slots, dec, back, rest_in, out, rest_out, acc, held, sem):
    position = lax.axis_index("tile")
    fetch = pltpu.make_async_copy(rest_in, held, sem.at[0])
    fetch.start()
    for b in range(BANDS):
        for o in range(2):
            acc[2 * b + o] = dec[b, o].astype(F32)
    fetch.wait()
    store = pltpu.make_async_copy(held, rest_out, sem.at[1])
    store.start()

    for s in range(CAP):

        def body(w, _):
            slot = slots[CAP * w + s]
            crop = jnp.maximum(slot, 0)
            row0 = boxes[0, crop]
            cols = pl.ds(boxes[1, crop], SPAN)
            for i in range(2):
                h = (2 * position + i - row0) & (STRIDE - 1)
                live = (slot >= 0) & (h < SPAN)
                row = jnp.where(live, 2 * ((row0 + h) >> 6) + i, 2 * BANDS + i)
                acc[row, cols, :] = acc[row, cols, :] + back[s, w, i].astype(F32)
            return 0

        lax.fori_loop(0, TILES, body, 0, unroll=2)
    for b in range(BANDS):
        for o in range(2):
            out[b, o] = acc[2 * b + o].astype(BF)
    store.wait()


def shards(
    features,
    dec_weight,
    dec_bias,
    first_weight,
    first_bias,
    second_weight,
    second_bias,
    boxes,
    slots,
):
    smem = pl.BlockSpec(memory_space=pltpu.SMEM)
    vmem = pl.BlockSpec(memory_space=pltpu.VMEM)
    any_ = pl.BlockSpec(memory_space=pl.ANY)
    rest_type = jax.ShapeDtypeStruct((CAP, S, S, C), BF)
    frame_type = jax.ShapeDtypeStruct(features.shape, BF)
    dma = pltpu.SemaphoreType.DMA
    pair = pltpu.VMEM((12 * C, 2 * C), BF)
    padded = pltpu.VMEM((S, S + 16, C), F32)
    spread = pltpu.VMEM((S // 2 + 1, 2, S, 3 * C), BF)
    sent = pltpu.VMEM((CAP, TILES, 2 * SENT, C), BF)

    decoded, rest, back = pl.pallas_call(
        main_kernel,
        out_shape=(
            frame_type,
            rest_type,
            jax.ShapeDtypeStruct((CAP, TILES, 2, SPAN, C), BF),
        ),
        in_specs=[smem, smem] + [vmem] * 7,
        out_specs=(any_, any_, any_),
        scratch_shapes=[
            pair,
            pair,
            pair,
            pltpu.VMEM((2 * BANDS, COLS + 16, C), F32),
            sent,
            sent,
            pltpu.VMEM((STRIDE + 1, SENT, C), F32),
            pltpu.VMEM((SPAN // 2 + 1, 2, SPAN, 3 * C), BF),
            pltpu.VMEM((SPAN, S, C), F32),
            padded,
            padded,
            spread,
            spread,
            pltpu.VMEM((S, S, C), F32),
            pltpu.VMEM((CAP, S, S, C), BF),
            pltpu.VMEM((CAP, TILES, 2, SPAN, C), BF),
            pltpu.VMEM((2, BANDS, COLS, C), BF),
            pltpu.VMEM((2, COLS + 16, C), F32),
            pltpu.VMEM((4, COLS, 3 * C), BF),
            pltpu.VMEM((BANDS, 2, COLS, C), BF),
            dma((CAP, PEERS)),
            dma((CAP, PEERS)),
            dma((CAP, PEERS)),
            dma((CAP, PEERS)),
            dma((2,)),
            dma((2,)),
            dma((7,)),
        ],
        compiler_params=pltpu.CompilerParams(
            collective_id=0, has_side_effects=True, vmem_limit_bytes=VMEM_LIMIT
        ),
        name="main",
    )(
        boxes,
        slots,
        features,
        dec_weight,
        dec_bias[None],
        first_weight,
        first_bias[None],
        second_weight,
        second_bias[None],
    )

    return pl.pallas_call(
        paste_kernel,
        out_shape=(frame_type, rest_type),
        in_specs=[smem, smem, vmem, vmem, any_],
        out_specs=(vmem, any_),
        scratch_shapes=[
            pltpu.VMEM((2 * BANDS + 2, COLS, C), F32),
            pltpu.VMEM((CAP, S, S, C), BF),
            dma((2,)),
        ],
        compiler_params=pltpu.CompilerParams(vmem_limit_bytes=VMEM_LIMIT),
        name="paste",
    )(boxes, slots, decoded, back, rest)


def solution(mesh):
    return jax.shard_map(
        shards,
        mesh=mesh,
        in_specs=(
            P("sess", "tile", None, None),
            P(),
            P(),
            P(),
            P(),
            P(),
            P(),
            P(None, "sess"),
            P("sess"),
        ),
        out_specs=(P("sess", "tile", None, None), P(("sess", "tile"), None, None, None)),
        check_vma=False,
    )
```

```python
import jax
import jax.numpy as jnp
from jax import lax
from jax.experimental import pallas as pl
from jax.experimental.pallas import tpu as pltpu
from jax.sharding import PartitionSpec as P

S = 64
UNIT = 12
SPAN = 48
C = 128
BANDS = 6
COLS = 320
STRIDE = 64
TILES = 32
CAP = 2
FRAME = BANDS * STRIDE
SENT = 56
MESH = pl.DeviceIdType.MESH
BF = jnp.bfloat16
F32 = jnp.float32
CHUNK = 4
U_DEC = 3
U_CONV1 = 2
U_CONV2 = 2
U_PATCH = 8
VMEM_LIMIT = 60 * 1024 * 1024

OFFSETS = sorted(
    [(dy, dx, dc) for dy in range(4) for dx in range(4) for dc in range(2) if dy + dx + dc],
    key=lambda d: -(min(d[0], 4 - d[0]) + min(d[1], 4 - d[1])),
)
PEERS = len(OFFSETS)


def silu(v):
    half = 0.5 * v
    return half + half * jnp.tanh(half)


def rounded(v):
    return v.astype(BF).astype(F32)


def pair_weight(w_ref, out_ref):
    zero = jnp.zeros((C, C), BF)
    for a in range(4):
        for dx in range(3):
            rows = pl.ds((a * 3 + dx) * C, C)
            out_ref[rows, 0:C] = w_ref[3 * a + dx] if a < 3 else zero
            out_ref[rows, C : 2 * C] = w_ref[3 * (a - 1) + dx] if a > 0 else zero


def widen(pad_ref, index, start, cols):
    return jnp.concatenate(
        [pad_ref[index, pl.ds(start + dx, cols), :].astype(BF) for dx in range(3)], axis=-1
    )


def spread_row(v):
    cell = lax.broadcasted_iota(jnp.int32, (8, C), 0)
    left = pltpu.roll(v, 1, 0)
    left = jnp.concatenate([jnp.where(cell == 0, 0.0, left[0:8]), left[8:]], axis=0)
    right = pltpu.roll(v, S - 1, 0)
    right = jnp.concatenate([right[: S - 8], jnp.where(cell == 7, 0.0, right[S - 8 :])], axis=0)
    return jnp.concatenate([left.astype(BF), v.astype(BF), right.astype(BF)], axis=-1)


def conv_pairs(wide, w_pair, bias, m0, cols):
    lhs = jnp.concatenate(
        [
            wide[pl.ds(m0 + a // 2, CHUNK), a % 2].reshape(CHUNK * cols, 3 * C)
            for a in range(4)
        ],
        axis=-1,
    )
    return jnp.dot(lhs, w_pair[...], preferred_element_type=F32) + bias


def twice(b_ref):
    return jnp.concatenate([b_ref[...], b_ref[...]], axis=-1)


def main_kernel(
    boxes,
    slots,
    feat,
    w0,
    b0,
    w1,
    b1,
    w2,
    b2,
    dec_out,
    rest_out,
    back,
    w0_pair,
    w1_pair,
    w2_pair,
    fpad,
    payload,
    got,
    reg,
    wide0,
    value,
    cut,
    wide,
    wide2,
    delta,
    rest,
    ret,
    halo,
    hpad,
    dwide,
    dec,
    fwd_send,
    fwd_recv,
    ret_send,
    ret_recv,
    halo_send,
    halo_recv,
    local_sem,
):
    me = lax.axis_index("tile")
    y, x, core = me // 8, (me // 2) % 4, me % 2
    targets = [
        ((y + dy) % 4) * 8 + ((x + dx) % 4) * 2 + (core + dc) % 2 for dy, dx, dc in OFFSETS
    ]
    barrier = pltpu.get_barrier_semaphore()
    for t in targets:
        pl.semaphore_signal(barrier, inc=1, device_id={"tile": t}, device_id_type=MESH)

    def remote(src, dst, send, recv, t):
        return pltpu.make_async_remote_copy(
            src_ref=src,
            dst_ref=dst,
            send_sem=send,
            recv_sem=recv,
            device_id={"tile": t},
            device_id_type=MESH,
        )

    def forward(s):
        return [
            remote(
                payload.at[s, t], got.at[s, me], fwd_send.at[s, k], fwd_recv.at[s, k], t
            )
            for k, t in enumerate(targets)
        ]

    def backward(s):
        return [
            remote(ret.at[s, t], back.at[s, me], ret_send.at[s, k], ret_recv.at[s, k], t)
            for k, t in enumerate(targets)
        ]

    def own_forward(s):
        return pltpu.make_async_copy(payload.at[s, me], got.at[s, me], local_sem.at[s])

    def own_backward(s):
        return pltpu.make_async_copy(ret.at[s, me], back.at[s, me], local_sem.at[2 + s])

    def keep_rest(s):
        return pltpu.make_async_copy(rest.at[s], rest_out.at[s], local_sem.at[4 + s])

    def rims():
        after, ahead = (me + 1) % TILES, (me + TILES - 1) % TILES
        return [
            remote(feat.at[:, 1], halo.at[0], halo_send.at[0], halo_recv.at[0], after),
            remote(feat.at[:, 0], halo.at[1], halo_send.at[1], halo_recv.at[1], ahead),
        ]

    fpad[:, 0:8, :] = jnp.zeros((2 * BANDS, 8, C), F32)
    fpad[:, COLS + 8 : COLS + 16, :] = jnp.zeros((2 * BANDS, 8, C), F32)
    for b in range(BANDS):
        for o in range(2):
            fpad[2 * b + o, 8 : COLS + 8, :] = feat[b, o].astype(F32)

    def fill(s):
        def body(w, _):
            crop = jnp.maximum(slots[CAP * w + s], 0)
            row0 = boxes[0, crop] - 1
            col0 = boxes[1, crop]
            parts = []
            for i in range(2):
                h = (2 * me + i - row0) & (STRIDE - 1)
                band = jnp.clip((row0 + h) >> 6, 0, BANDS - 1)
                parts.append(fpad[2 * band + i, pl.ds(col0 + 7, SENT), :])
            payload[s, w] = jnp.concatenate(parts, axis=0).astype(BF)
            return 0

        lax.fori_loop(0, TILES, body, 0, unroll=2)

    fill(0)
    pl.semaphore_wait(barrier, PEERS)
    for copy in forward(0):
        copy.start()
    own_forward(0).start()
    fill(1)
    for copy in forward(1):
        copy.start()
    own_forward(1).start()
    for copy in rims():
        copy.start()

    pair_weight(w0, w0_pair)
    pair_weight(w1, w1_pair)
    pair_weight(w2, w2_pair)
    for ref in (wide, wide2):
        ref[0, 0] = jnp.zeros((S, 3 * C), BF)
        ref[S // 2, 1] = jnp.zeros((S, 3 * C), BF)
    reg[STRIDE] = jnp.zeros((SENT, C), F32)
    hpad[:, 0:8, :] = jnp.zeros((2, 8, C), F32)
    hpad[:, COLS + 8 : COLS + 16, :] = jnp.zeros((2, 8, C), F32)
    bias0, bias1, bias2 = twice(b0), twice(b1), twice(b2)

    def restore(s, _):
        own_forward(s).wait()
        for copy in forward(s):
            copy.wait_recv()
        slot = slots[CAP * me + s]
        crop = jnp.maximum(slot, 0)
        row0 = boxes[0, crop]
        side = UNIT * (boxes[2, crop] + 2)
        sidef = side.astype(F32)

        def unpack(p, _):
            block = got[s, p].astype(F32)
            reg[2 * p] = block[0:SENT]
            reg[2 * p + 1] = block[SENT : 2 * SENT]
            return 0

        lax.fori_loop(0, TILES, unpack, 0, unroll=8)

        def region(h, _):
            for o in range(2):
                row = row0 - 1 + 2 * h + o
                live = (row >= 0) & (row < FRAME)
                index = jnp.where(live, row & (STRIDE - 1), STRIDE)
                wide0[h, o] = widen(reg, index, 0, SPAN)
            return 0

        lax.fori_loop(0, SPAN // 2 + 1, region, 0, unroll=5)

        spot = (lax.broadcasted_iota(jnp.int32, (S, SPAN), 0).astype(F32) + 0.5) * sidef / S
        spot = jnp.clip(spot - 0.5, 0.0, sidef - 1.0)
        cell = lax.broadcasted_iota(jnp.int32, (S, SPAN), 1).astype(F32)
        down = jnp.maximum(0.0, 1.0 - jnp.abs(spot - cell)).astype(BF)

        def decode(j, _):
            m0 = j * CHUNK
            act = silu(conv_pairs(wide0, w0_pair, bias0, m0, SPAN))
            act = act.reshape(CHUNK, SPAN, 2 * C)
            for i in range(CHUNK):
                centre = jnp.concatenate(
                    [wide0[m0 + i, 1, :, C : 2 * C], wide0[m0 + i + 1, 0, :, C : 2 * C]], axis=-1
                )
                value[m0 + i] = (centre.astype(F32) + act[i]).astype(BF)
            return 0

        lax.fori_loop(0, SPAN // 2 // CHUNK, decode, 0, unroll=U_DEC)

        def colcut(m, _):
            z = rounded(jnp.dot(down, value[m], preferred_element_type=F32))
            cut[2 * m] = z[:, 0:C]
            cut[2 * m + 1] = z[:, C : 2 * C]
            return 0

        lax.fori_loop(0, SPAN // 2, colcut, 0, unroll=12)

        def crop_row(t, _):
            num = jnp.clip((2 * t + 1) * side - S, 0, (side - 1) * 128)
            first = num >> 7
            second = jnp.minimum(first + 1, SPAN - 1)
            frac = (num & 127).astype(F32) * (1.0 / 128.0)
            v = (1.0 - frac) * cut[first] + frac * cut[second]
            wide[(t + 1) >> 1, (t + 1) & 1] = spread_row(v)
            return 0

        lax.fori_loop(0, S, crop_row, 0, unroll=8)
        groups = S // (2 * CHUNK)

        def first_conv(j, _):
            v = silu(conv_pairs(wide, w1_pair, bias1, j * CHUNK, S))
            v = v.reshape(CHUNK, S, 2 * C)
            for i in range(CHUNK):
                wide2[j * CHUNK + i, 1] = spread_row(v[i, :, 0:C])
                wide2[j * CHUNK + i + 1, 0] = spread_row(v[i, :, C : 2 * C])
            return 0

        lax.fori_loop(0, groups, first_conv, 0, unroll=U_CONV1)
        keep = slot >= 0

        def second_conv(j, _):
            v = rounded(conv_pairs(wide2, w2_pair, bias2, j * CHUNK, S))
            v = v.reshape(CHUNK, S, 2 * C)
            for i in range(CHUNK):
                for o in range(2):
                    row = 2 * (j * CHUNK + i) + o
                    part = v[i, :, o * C : (o + 1) * C]
                    delta[row] = part
                    rest[s, row] = jnp.where(keep, part, 0.0).astype(BF)
            return 0

        lax.fori_loop(0, groups, second_conv, 0, unroll=U_CONV2)
        keep_rest(s).start()

        where = (lax.broadcasted_iota(jnp.int32, (SPAN, S), 0).astype(F32) + 0.5) * S / sidef
        where = jnp.clip(where - 0.5, 0.0, S - 1.0)
        inside = lax.broadcasted_iota(jnp.int32, (SPAN, S), 0) < side
        grid = lax.broadcasted_iota(jnp.int32, (SPAN, S), 1).astype(F32)
        lift = jnp.where(inside, jnp.maximum(0.0, 1.0 - jnp.abs(where - grid)), 0.0)
        lift_high = lift.astype(BF)
        lift_low = (lift - lift_high.astype(F32)).astype(BF)
        lifts = jnp.concatenate([lift_high, lift_low], axis=0)
        magic = jnp.where(side == 24, 10923, jnp.where(side == 36, 7282, 5462))
        inverse = jnp.where(side == 24, 1.0 / 24, jnp.where(side == 36, 1.0 / 36, 1.0 / 48))

        def patch(p):
            halves = []
            for i in range(2):
                h = (2 * p + i - row0) & (STRIDE - 1)
                num = jnp.clip((2 * h + 1) * (S // 2) - (side >> 1), 0, (S - 1) * side)
                one = (num * magic) >> 18
                frac = (num - one * side).astype(F32) * inverse
                live = (h < side).astype(F32)
                two = jnp.minimum(one + 1, S - 1)
                halves.append(
                    ((live - live * frac) * delta[one] + (live * frac) * delta[two]).astype(BF)
                )
            rhs = jnp.concatenate(halves, axis=-1)
            z = jnp.dot(lifts, rhs, preferred_element_type=F32)
            z = (z[0:SPAN] + z[SPAN : 2 * SPAN]).astype(BF)
            ret[s, p, 0] = z[:, 0:C]
            ret[s, p, 1] = z[:, C : 2 * C]

        copies = backward(s)
        for k0 in range(0, PEERS + 1, U_PATCH):
            for t in (targets + [me])[k0 : k0 + U_PATCH]:
                patch(t)
            for copy in copies[max(k0 - U_PATCH, 0) : k0]:
                copy.start()
        for copy in copies[PEERS + 1 - U_PATCH :]:
            copy.start()
        own_backward(s).start()
        return 0

    lax.fori_loop(0, CAP, restore, 0)

    for copy in rims():
        copy.wait_recv()

    def band(b, _):
        up = jnp.where(me == 0, b - 1, b)
        low = jnp.where(me == TILES - 1, b + 1, b)
        up_ok = (up >= 0).astype(F32)
        low_ok = (low < BANDS).astype(F32)
        hpad[0, 8 : COLS + 8, :] = halo[0, jnp.maximum(up, 0)].astype(F32) * up_ok
        hpad[1, 8 : COLS + 8, :] = halo[1, jnp.minimum(low, BANDS - 1)].astype(F32) * low_ok
        dwide[0] = widen(hpad, 0, 7, COLS)
        dwide[1] = widen(fpad, 2 * b, 7, COLS)
        dwide[2] = widen(fpad, 2 * b + 1, 7, COLS)
        dwide[3] = widen(hpad, 1, 7, COLS)
        for part in range(2):
            rows = pl.ds(part * (COLS // 2), COLS // 2)
            lhs = jnp.concatenate([dwide[a, rows, :] for a in range(4)], axis=-1)
            act = silu(jnp.dot(lhs, w0_pair[...], preferred_element_type=F32) + bias0)
            for o in range(2):
                v = feat[b, o, rows, :].astype(F32) + act[:, o * C : (o + 1) * C]
                dec[b, o, rows, :] = v.astype(BF)
        return 0

    lax.fori_loop(0, BANDS, band, 0)
    out = pltpu.make_async_copy(dec, dec_out, local_sem.at[6])
    out.start()
    for copy in rims():
        copy.wait_send()
    for s in range(CAP):
        for copy in forward(s):
            copy.wait_send()
        keep_rest(s).wait()
        own_backward(s).wait()
    for s in range(CAP):
        for copy in backward(s):
            copy.wait()
    out.wait()


def paste_kernel(
    boxes, slots, dec_in, back_in, rest_in, out, rest_out, dec, back, rest, acc, done, sem
):
    position = lax.axis_index("tile")
    fetch_dec = pltpu.make_async_copy(dec_in, dec, sem.at[0])
    fetch_back = [
        pltpu.make_async_copy(back_in.at[s], back.at[s], sem.at[1 + s]) for s in range(CAP)
    ]
    fetch_rest = pltpu.make_async_copy(rest_in, rest, sem.at[3])
    store_rest = pltpu.make_async_copy(rest, rest_out, sem.at[4])
    fetch_dec.start()
    for copy in fetch_back:
        copy.start()
    fetch_rest.start()
    fetch_dec.wait()
    for b in range(BANDS):
        for o in range(2):
            acc[2 * b + o] = dec[b, o].astype(F32)

    for s in range(CAP):
        fetch_back[s].wait()

        def body(w, _):
            slot = slots[CAP * w + s]

            @pl.when(slot >= 0)
            def _():
                row0 = boxes[0, slot]
                cols = pl.ds(boxes[1, slot], SPAN)
                for i in range(2):
                    h = (2 * position + i - row0) & (STRIDE - 1)
                    row = jnp.where(h < SPAN, 2 * ((row0 + h) >> 6) + i, 2 * BANDS + i)
                    acc[row, cols, :] = acc[row, cols, :] + back[s, w, i].astype(F32)

            return 0

        lax.fori_loop(0, TILES, body, 0)
        if s == 0:
            fetch_rest.wait()
            store_rest.start()
    stores = []
    for b in range(BANDS):
        for o in range(2):
            done[b, o] = acc[2 * b + o].astype(BF)
        stores.append(pltpu.make_async_copy(done.at[b], out.at[b], sem.at[5 + b]))
        stores[-1].start()
    store_rest.wait()
    for copy in stores:
        copy.wait()


def shards(
    features,
    dec_weight,
    dec_bias,
    first_weight,
    first_bias,
    second_weight,
    second_bias,
    boxes,
    slots,
):
    smem = pl.BlockSpec(memory_space=pltpu.SMEM)
    vmem = pl.BlockSpec(memory_space=pltpu.VMEM)
    any_ = pl.BlockSpec(memory_space=pl.ANY)
    rest_type = jax.ShapeDtypeStruct((CAP, S, S, C), BF)
    frame_type = jax.ShapeDtypeStruct(features.shape, BF)
    dma = pltpu.SemaphoreType.DMA
    pair = pltpu.VMEM((12 * C, 2 * C), BF)
    spread = pltpu.VMEM((S // 2 + 1, 2, S, 3 * C), BF)
    sent = pltpu.VMEM((CAP, TILES, 2 * SENT, C), BF)

    decoded, rest, back = pl.pallas_call(
        main_kernel,
        out_shape=(
            frame_type,
            rest_type,
            jax.ShapeDtypeStruct((CAP, TILES, 2, SPAN, C), BF),
        ),
        in_specs=[smem, smem] + [vmem] * 7,
        out_specs=(any_, any_, any_),
        scratch_shapes=[
            pair,
            pair,
            pair,
            pltpu.VMEM((2 * BANDS, COLS + 16, C), F32),
            sent,
            sent,
            pltpu.VMEM((STRIDE + 1, SENT, C), F32),
            pltpu.VMEM((SPAN // 2 + 1, 2, SPAN, 3 * C), BF),
            pltpu.VMEM((SPAN // 2, SPAN, 2 * C), BF),
            pltpu.VMEM((SPAN, S, C), F32),
            spread,
            spread,
            pltpu.VMEM((S, S, C), F32),
            pltpu.VMEM((CAP, S, S, C), BF),
            pltpu.VMEM((CAP, TILES, 2, SPAN, C), BF),
            pltpu.VMEM((2, BANDS, COLS, C), BF),
            pltpu.VMEM((2, COLS + 16, C), F32),
            pltpu.VMEM((4, COLS, 3 * C), BF),
            pltpu.VMEM((BANDS, 2, COLS, C), BF),
            dma((CAP, PEERS)),
            dma((CAP, PEERS)),
            dma((CAP, PEERS)),
            dma((CAP, PEERS)),
            dma((2,)),
            dma((2,)),
            dma((7,)),
        ],
        compiler_params=pltpu.CompilerParams(
            collective_id=0, has_side_effects=True, vmem_limit_bytes=VMEM_LIMIT
        ),
        name="main",
    )(
        boxes,
        slots,
        features,
        dec_weight,
        dec_bias[None],
        first_weight,
        first_bias[None],
        second_weight,
        second_bias[None],
    )

    return pl.pallas_call(
        paste_kernel,
        out_shape=(frame_type, rest_type),
        in_specs=[smem, smem, any_, any_, any_],
        out_specs=(any_, any_),
        scratch_shapes=[
            pltpu.VMEM((BANDS, 2, COLS, C), BF),
            pltpu.VMEM((CAP, TILES, 2, SPAN, C), BF),
            pltpu.VMEM((CAP, S, S, C), BF),
            pltpu.VMEM((2 * BANDS + 2, COLS, C), F32),
            pltpu.VMEM((BANDS, 2, COLS, C), BF),
            dma((5 + BANDS,)),
        ],
        compiler_params=pltpu.CompilerParams(vmem_limit_bytes=VMEM_LIMIT),
        name="paste",
    )(boxes, slots, decoded, back, rest)


def solution(mesh):
    return jax.shard_map(
        shards,
        mesh=mesh,
        in_specs=(
            P("sess", "tile", None, None),
            P(),
            P(),
            P(),
            P(),
            P(),
            P(),
            P(None, "sess"),
            P("sess"),
        ),
        out_specs=(P("sess", "tile", None, None), P(("sess", "tile"), None, None, None)),
        check_vma=False,
    )
```

```python
import jax
import jax.numpy as jnp
from jax import lax
from jax.experimental import pallas as pl
from jax.experimental.pallas import tpu as pltpu
from jax.sharding import PartitionSpec as P

S = 64
UNIT = 12
SPAN = 48
C = 128
BANDS = 6
COLS = 320
STRIDE = 64
TILES = 32
CAP = 2
FRAME = BANDS * STRIDE
RIMMED = SPAN + 2
SENT = 104
MESH = pl.DeviceIdType.MESH
BF = jnp.bfloat16
F32 = jnp.float32
CHUNK = 4
U_DEC = 2
U_CONV1 = 2
U_CONV2 = 4
U_PATCH = 16
VMEM_LIMIT = 60 * 1024 * 1024

OFFSETS = sorted(
    [(dy, dx, dc) for dy in range(4) for dx in range(4) for dc in range(2) if dy + dx + dc],
    key=lambda d: -(min(d[0], 4 - d[0]) + min(d[1], 4 - d[1])),
)
PEERS = len(OFFSETS)


def silu(v):
    half = 0.5 * v
    return half + half * jnp.tanh(half)


def rounded(v):
    return v.astype(BF).astype(F32)


def pair_weight(w_ref, out_ref):
    zero = jnp.zeros((C, C), BF)
    for a in range(4):
        for dx in range(3):
            rows = pl.ds((a * 3 + dx) * C, C)
            out_ref[rows, 0:C] = w_ref[3 * a + dx] if a < 3 else zero
            out_ref[rows, C : 2 * C] = w_ref[3 * (a - 1) + dx] if a > 0 else zero


def widen(pad_ref, index, start, cols):
    return jnp.concatenate(
        [pad_ref[index, pl.ds(start + dx, cols), :].astype(BF) for dx in range(3)], axis=-1
    )


def spread_row(v):
    cell = lax.broadcasted_iota(jnp.int32, (8, C), 0)
    left = pltpu.roll(v, 1, 0)
    left = jnp.concatenate([jnp.where(cell == 0, 0.0, left[0:8]), left[8:]], axis=0)
    right = pltpu.roll(v, S - 1, 0)
    right = jnp.concatenate([right[: S - 8], jnp.where(cell == 7, 0.0, right[S - 8 :])], axis=0)
    return jnp.concatenate([left.astype(BF), v.astype(BF), right.astype(BF)], axis=-1)


def conv_pairs(wide, w_pair, bias, m0, cols):
    lhs = jnp.concatenate(
        [
            wide[pl.ds(m0 + a // 2, CHUNK), a % 2].reshape(CHUNK * cols, 3 * C)
            for a in range(4)
        ],
        axis=-1,
    )
    return jnp.dot(lhs, w_pair[...], preferred_element_type=F32) + bias


def twice(b_ref):
    return jnp.concatenate([b_ref[...], b_ref[...]], axis=-1)


def main_kernel(
    boxes,
    slots,
    feat_in,
    w0_in,
    b0,
    w1_in,
    b1,
    w2_in,
    b2,
    dec_out,
    rest_out,
    back,
    feat,
    w0,
    w1,
    w2,
    w0_pair,
    w1_pair,
    w2_pair,
    fpad,
    stage,
    payload,
    got,
    reg,
    wide0,
    value,
    cut,
    wide,
    wide2,
    delta,
    rest,
    ret,
    halo,
    hpad,
    dwide,
    dec,
    crop_tap,
    crop_frac,
    back_tap,
    back_one,
    back_two,
    fwd_send,
    fwd_recv,
    ret_send,
    ret_recv,
    halo_send,
    halo_recv,
    local_sem,
    load_sem,
):
    fetches = [
        pltpu.make_async_copy(feat_in.at[b], feat.at[b], load_sem.at[3 + b]) for b in range(BANDS)
    ]
    for fetch in fetches:
        fetch.start()
    me = lax.axis_index("tile")
    y, x, core = me // 8, (me // 2) % 4, me % 2
    targets = [
        ((y + dy) % 4) * 8 + ((x + dx) % 4) * 2 + (core + dc) % 2 for dy, dx, dc in OFFSETS
    ]
    barrier = pltpu.get_barrier_semaphore()
    for t in targets:
        pl.semaphore_signal(barrier, inc=1, device_id={"tile": t}, device_id_type=MESH)

    def remote(src, dst, send, recv, t):
        return pltpu.make_async_remote_copy(
            src_ref=src,
            dst_ref=dst,
            send_sem=send,
            recv_sem=recv,
            device_id={"tile": t},
            device_id_type=MESH,
        )

    def forward(s):
        return [
            remote(
                payload.at[s, t], got.at[s, me], fwd_send.at[s, k], fwd_recv.at[s, k], t
            )
            for k, t in enumerate(targets)
        ]

    def backward(s):
        return [
            remote(ret.at[s, t], back.at[s, me], ret_send.at[s, k], ret_recv.at[s, k], t)
            for k, t in enumerate(targets)
        ]

    def own_forward(s):
        return pltpu.make_async_copy(payload.at[s, me], got.at[s, me], local_sem.at[s])

    def own_backward(s):
        return pltpu.make_async_copy(ret.at[s, me], back.at[s, me], local_sem.at[2 + s])

    def keep_rest(s):
        return pltpu.make_async_copy(rest.at[s], rest_out.at[s], local_sem.at[4 + s])

    def rims():
        after, ahead = (me + 1) % TILES, (me + TILES - 1) % TILES
        return [
            remote(feat.at[:, 1], halo.at[0], halo_send.at[0], halo_recv.at[0], after),
            remote(feat.at[:, 0], halo.at[1], halo_send.at[1], halo_recv.at[1], ahead),
        ]

    loads = [
        pltpu.make_async_copy(src, dst, load_sem.at[k])
        for k, (src, dst) in enumerate(((w0_in, w0), (w1_in, w1), (w2_in, w2)))
    ]
    for load in loads:
        load.start()
    fpad[:, 0:8, :] = jnp.zeros((2 * BANDS, 8, C), F32)
    fpad[:, COLS + 8 : COLS + 16, :] = jnp.zeros((2 * BANDS, 8, C), F32)
    for b in range(BANDS):
        fetches[b].wait()
        for o in range(2):
            fpad[2 * b + o, 8 : COLS + 8, :] = feat[b, o].astype(F32)

    def fill(s, w, spot):
        crop = jnp.maximum(slots[CAP * w + s], 0)
        row0 = boxes[0, crop] - 1
        col0 = boxes[1, crop]
        for i in range(2):
            h = (2 * me + i - row0) & (STRIDE - 1)
            band = jnp.clip((row0 + h) >> 6, 0, BANDS - 1)
            stage[spot, pl.ds(i * RIMMED, 56), :] = fpad[2 * band + i, pl.ds(col0 + 7, 56), :]
        payload[s, w] = stage[spot, 0:SENT].astype(BF)

    ahead = forward(0)
    step = 4
    for k0 in range(0, PEERS + 1, step):
        for k, w in enumerate((targets + [me])[k0 : k0 + step]):
            fill(0, w, k)
        if k0 == step:
            pl.semaphore_wait(barrier, PEERS)
        for copy in ahead[max(k0 - step, 0) : k0]:
            copy.start()
    for copy in ahead[PEERS + 1 - step :]:
        copy.start()
    own_forward(0).start()

    def fill_next(j, _):
        for k in range(4):
            fill(1, 4 * j + k, k)
        return 0

    lax.fori_loop(0, TILES // 4, fill_next, 0)
    for load in loads:
        load.wait()
    pair_weight(w0, w0_pair)
    pair_weight(w1, w1_pair)
    pair_weight(w2, w2_pair)
    for ref in (wide, wide2):
        ref[0, 0] = jnp.zeros((S, 3 * C), BF)
        ref[S // 2, 1] = jnp.zeros((S, 3 * C), BF)
    reg[TILES] = jnp.zeros((SENT, C), F32)
    def taps(k, _):
        crop = jnp.maximum(slots[CAP * me + k // S], 0)
        side = UNIT * (boxes[2, crop] + 2)
        t = k % S
        num = jnp.clip((2 * t + 1) * side - S, 0, (side - 1) * 128)
        crop_tap[k] = num >> 7
        crop_frac[k] = (num & 127).astype(F32) * (1.0 / 128.0)
        h = (t - boxes[0, crop]) & (STRIDE - 1)
        magic = jnp.where(side == 24, 10923, jnp.where(side == 36, 7282, 5462))
        inverse = jnp.where(side == 24, 1.0 / 24, jnp.where(side == 36, 1.0 / 36, 1.0 / 48))
        num = jnp.clip((2 * h + 1) * (S // 2) - (side >> 1), 0, (S - 1) * side)
        one = (num * magic) >> 18
        frac = (num - one * side).astype(F32) * inverse
        live = (h < side).astype(F32)
        back_tap[k] = one
        back_one[k] = live - live * frac
        back_two[k] = live * frac
        return 0

    lax.fori_loop(0, CAP * S, taps, 0, unroll=4)
    hpad[:, 0:8, :] = jnp.zeros((2, 8, C), F32)
    hpad[:, COLS + 8 : COLS + 16, :] = jnp.zeros((2, 8, C), F32)
    bias0, bias1, bias2 = twice(b0), twice(b1), twice(b2)

    def arrived(s):
        own_forward(s).wait()
        for copy in forward(s):
            copy.wait_recv()

    arrived(0)
    for copy in forward(1):
        copy.start()
    own_forward(1).start()
    for copy in rims():
        copy.start()

    def restore(s, _):
        slot = slots[CAP * me + s]
        crop = jnp.maximum(slot, 0)
        row0 = boxes[0, crop]
        side = UNIT * (boxes[2, crop] + 2)
        sidef = side.astype(F32)

        def unpack(p, _):
            reg[p] = got[s, p].astype(F32)
            return 0

        lax.fori_loop(0, TILES, unpack, 0, unroll=8)

        def region(h, _):
            for o in range(2):
                row = row0 - 1 + 2 * h + o
                live = (row >= 0) & (row < FRAME)
                index = jnp.where(live, (row & (STRIDE - 1)) >> 1, TILES)
                wide0[h, o] = widen(reg, index, (row & 1) * RIMMED, SPAN)
            return 0

        lax.fori_loop(0, SPAN // 2 + 1, region, 0, unroll=5)

        spot = (lax.broadcasted_iota(jnp.int32, (S, SPAN), 0).astype(F32) + 0.5) * sidef / S
        spot = jnp.clip(spot - 0.5, 0.0, sidef - 1.0)
        cell = lax.broadcasted_iota(jnp.int32, (S, SPAN), 1).astype(F32)
        down = jnp.maximum(0.0, 1.0 - jnp.abs(spot - cell)).astype(BF)

        def decode(j, _):
            m0 = j * CHUNK
            act = silu(conv_pairs(wide0, w0_pair, bias0, m0, SPAN))
            act = act.reshape(CHUNK, SPAN, 2 * C)
            for i in range(CHUNK):
                centre = jnp.concatenate(
                    [wide0[m0 + i, 1, :, C : 2 * C], wide0[m0 + i + 1, 0, :, C : 2 * C]], axis=-1
                )
                value[m0 + i] = (centre.astype(F32) + act[i]).astype(BF)
            return 0

        lax.fori_loop(0, SPAN // 2 // CHUNK, decode, 0, unroll=U_DEC)

        def colcut(m, _):
            z = rounded(jnp.dot(down, value[m], preferred_element_type=F32))
            cut[2 * m] = z[:, 0:C]
            cut[2 * m + 1] = z[:, C : 2 * C]
            return 0

        lax.fori_loop(0, SPAN // 2, colcut, 0, unroll=12)

        def crop_row(t, _):
            first = crop_tap[s * S + t]
            second = jnp.minimum(first + 1, SPAN - 1)
            frac = crop_frac[s * S + t]
            v = (1.0 - frac) * cut[first] + frac * cut[second]
            wide[(t + 1) >> 1, (t + 1) & 1] = spread_row(v)
            return 0

        lax.fori_loop(0, S, crop_row, 0, unroll=8)
        groups = S // (2 * CHUNK)

        def first_conv(j, _):
            v = silu(conv_pairs(wide, w1_pair, bias1, j * CHUNK, S))
            v = v.reshape(CHUNK, S, 2 * C)
            for i in range(CHUNK):
                wide2[j * CHUNK + i, 1] = spread_row(v[i, :, 0:C])
                wide2[j * CHUNK + i + 1, 0] = spread_row(v[i, :, C : 2 * C])
            return 0

        lax.fori_loop(0, groups, first_conv, 0, unroll=U_CONV1)
        keep = slot >= 0

        def second_conv(j, _):
            v = rounded(conv_pairs(wide2, w2_pair, bias2, j * CHUNK, S))
            v = v.reshape(CHUNK, S, 2 * C)
            for i in range(CHUNK):
                for o in range(2):
                    row = 2 * (j * CHUNK + i) + o
                    part = v[i, :, o * C : (o + 1) * C]
                    delta[row] = part
                    rest[s, row] = jnp.where(keep, part, 0.0).astype(BF)
            return 0

        lax.fori_loop(0, groups, second_conv, 0, unroll=U_CONV2)
        keep_rest(s).start()

        where = (lax.broadcasted_iota(jnp.int32, (SPAN, S), 0).astype(F32) + 0.5) * S / sidef
        where = jnp.clip(where - 0.5, 0.0, S - 1.0)
        inside = lax.broadcasted_iota(jnp.int32, (SPAN, S), 0) < side
        grid = lax.broadcasted_iota(jnp.int32, (SPAN, S), 1).astype(F32)
        lift = jnp.where(inside, jnp.maximum(0.0, 1.0 - jnp.abs(where - grid)), 0.0)
        lift_high = lift.astype(BF)
        lift_low = (lift - lift_high.astype(F32)).astype(BF)
        lifts = jnp.concatenate([lift_high, lift_low], axis=0)
        def patch(p):
            halves = []
            for i in range(2):
                k = s * S + 2 * p + i
                one = back_tap[k]
                two = jnp.minimum(one + 1, S - 1)
                halves.append((back_one[k] * delta[one] + back_two[k] * delta[two]).astype(BF))
            rhs = jnp.concatenate(halves, axis=-1)
            z = jnp.dot(lifts, rhs, preferred_element_type=F32)
            z = (z[0:SPAN] + z[SPAN : 2 * SPAN]).astype(BF)
            ret[s, p, 0] = z[:, 0:C]
            ret[s, p, 1] = z[:, C : 2 * C]

        copies = backward(s)
        for k0 in range(0, PEERS + 1, U_PATCH):
            for t in (targets + [me])[k0 : k0 + U_PATCH]:
                patch(t)
            for copy in copies[max(k0 - U_PATCH, 0) : k0]:
                copy.start()
        for copy in copies[PEERS + 1 - U_PATCH :]:
            copy.start()
        own_backward(s).start()

        @pl.when(s == 0)
        def _():
            arrived(1)

        return 0

    lax.fori_loop(0, CAP, restore, 0)

    for copy in rims():
        copy.wait_recv()

    def band(b, _):
        up = jnp.where(me == 0, b - 1, b)
        low = jnp.where(me == TILES - 1, b + 1, b)
        up_ok = (up >= 0).astype(F32)
        low_ok = (low < BANDS).astype(F32)
        hpad[0, 8 : COLS + 8, :] = halo[0, jnp.maximum(up, 0)].astype(F32) * up_ok
        hpad[1, 8 : COLS + 8, :] = halo[1, jnp.minimum(low, BANDS - 1)].astype(F32) * low_ok
        dwide[0] = widen(hpad, 0, 7, COLS)
        dwide[1] = widen(fpad, 2 * b, 7, COLS)
        dwide[2] = widen(fpad, 2 * b + 1, 7, COLS)
        dwide[3] = widen(hpad, 1, 7, COLS)
        for part in range(2):
            rows = pl.ds(part * (COLS // 2), COLS // 2)
            lhs = jnp.concatenate([dwide[a, rows, :] for a in range(4)], axis=-1)
            act = silu(jnp.dot(lhs, w0_pair[...], preferred_element_type=F32) + bias0)
            for o in range(2):
                v = feat[b, o, rows, :].astype(F32) + act[:, o * C : (o + 1) * C]
                dec[b, o, rows, :] = v.astype(BF)
        return 0

    lax.fori_loop(0, BANDS, band, 0)
    out = pltpu.make_async_copy(dec, dec_out, local_sem.at[6])
    out.start()
    for copy in rims():
        copy.wait_send()
    for s in range(CAP):
        for copy in forward(s):
            copy.wait_send()
        keep_rest(s).wait()
        own_backward(s).wait()
    for s in range(CAP):
        for copy in backward(s):
            copy.wait()
    out.wait()


def paste_kernel(
    boxes, slots, dec_in, back_in, rest_in, out, rest_out, dec, back, rest, acc, done, sem
):
    position = lax.axis_index("tile")
    fetch_dec = pltpu.make_async_copy(dec_in, dec, sem.at[0])
    fetch_back = [
        pltpu.make_async_copy(back_in.at[s], back.at[s], sem.at[1 + s]) for s in range(CAP)
    ]
    fetch_rest = pltpu.make_async_copy(rest_in, rest, sem.at[3])
    store_rest = pltpu.make_async_copy(rest, rest_out, sem.at[4])
    fetch_dec.start()
    for copy in fetch_back:
        copy.start()
    fetch_rest.start()
    fetch_dec.wait()
    for b in range(BANDS):
        for o in range(2):
            acc[2 * b + o] = dec[b, o].astype(F32)

    for s in range(CAP):
        fetch_back[s].wait()

        def body(w, _):
            slot = slots[CAP * w + s]

            @pl.when(slot >= 0)
            def _():
                row0 = boxes[0, slot]
                cols = pl.ds(boxes[1, slot], SPAN)
                for i in range(2):
                    h = (2 * position + i - row0) & (STRIDE - 1)
                    row = jnp.where(h < SPAN, 2 * ((row0 + h) >> 6) + i, 2 * BANDS + i)
                    acc[row, cols, :] = acc[row, cols, :] + back[s, w, i].astype(F32)

            return 0

        lax.fori_loop(0, TILES, body, 0)
        if s == 0:
            fetch_rest.wait()
            store_rest.start()
    stores = []
    for b in range(BANDS):
        for o in range(2):
            done[b, o] = acc[2 * b + o].astype(BF)
        stores.append(pltpu.make_async_copy(done.at[b], out.at[b], sem.at[5 + b]))
        stores[-1].start()
    store_rest.wait()
    for copy in stores:
        copy.wait()


def shards(
    features,
    dec_weight,
    dec_bias,
    first_weight,
    first_bias,
    second_weight,
    second_bias,
    boxes,
    slots,
):
    smem = pl.BlockSpec(memory_space=pltpu.SMEM)
    vmem = pl.BlockSpec(memory_space=pltpu.VMEM)
    any_ = pl.BlockSpec(memory_space=pl.ANY)
    rest_type = jax.ShapeDtypeStruct((CAP, S, S, C), BF)
    frame_type = jax.ShapeDtypeStruct(features.shape, BF)
    dma = pltpu.SemaphoreType.DMA
    pair = pltpu.VMEM((12 * C, 2 * C), BF)
    spread = pltpu.VMEM((S // 2 + 1, 2, S, 3 * C), BF)
    table = (CAP * S,)
    sent = pltpu.VMEM((CAP, TILES, SENT, C), BF)
    weight = pltpu.VMEM((9, C, C), BF)

    decoded, rest, back = pl.pallas_call(
        main_kernel,
        out_shape=(
            frame_type,
            rest_type,
            jax.ShapeDtypeStruct((CAP, TILES, 2, SPAN, C), BF),
        ),
        in_specs=[smem, smem, any_] + [any_, vmem] * 3,
        out_specs=(any_, any_, any_),
        scratch_shapes=[
            pltpu.VMEM((BANDS, 2, COLS, C), BF),
            weight,
            weight,
            weight,
            pair,
            pair,
            pair,
            pltpu.VMEM((2 * BANDS, COLS + 16, C), F32),
            pltpu.VMEM((4, SENT + 8, C), F32),
            sent,
            sent,
            pltpu.VMEM((TILES + 1, SENT, C), F32),
            pltpu.VMEM((SPAN // 2 + 1, 2, SPAN, 3 * C), BF),
            pltpu.VMEM((SPAN // 2, SPAN, 2 * C), BF),
            pltpu.VMEM((SPAN, S, C), F32),
            spread,
            spread,
            pltpu.VMEM((S, S, C), F32),
            pltpu.VMEM((CAP, S, S, C), BF),
            pltpu.VMEM((CAP, TILES, 2, SPAN, C), BF),
            pltpu.VMEM((2, BANDS, COLS, C), BF),
            pltpu.VMEM((2, COLS + 16, C), F32),
            pltpu.VMEM((4, COLS, 3 * C), BF),
            pltpu.VMEM((BANDS, 2, COLS, C), BF),
            pltpu.SMEM(table, jnp.int32),
            pltpu.SMEM(table, F32),
            pltpu.SMEM(table, jnp.int32),
            pltpu.SMEM(table, F32),
            pltpu.SMEM(table, F32),
            dma((CAP, PEERS)),
            dma((CAP, PEERS)),
            dma((CAP, PEERS)),
            dma((CAP, PEERS)),
            dma((2,)),
            dma((2,)),
            dma((7,)),
            dma((3 + BANDS,)),
        ],
        compiler_params=pltpu.CompilerParams(
            collective_id=0, has_side_effects=True, vmem_limit_bytes=VMEM_LIMIT
        ),
        name="main",
    )(
        boxes,
        slots,
        features,
        dec_weight,
        dec_bias[None],
        first_weight,
        first_bias[None],
        second_weight,
        second_bias[None],
    )

    return pl.pallas_call(
        paste_kernel,
        out_shape=(frame_type, rest_type),
        in_specs=[smem, smem, any_, any_, any_],
        out_specs=(any_, any_),
        scratch_shapes=[
            pltpu.VMEM((BANDS, 2, COLS, C), BF),
            pltpu.VMEM((CAP, TILES, 2, SPAN, C), BF),
            pltpu.VMEM((CAP, S, S, C), BF),
            pltpu.VMEM((2 * BANDS + 2, COLS, C), F32),
            pltpu.VMEM((BANDS, 2, COLS, C), BF),
            dma((5 + BANDS,)),
        ],
        compiler_params=pltpu.CompilerParams(vmem_limit_bytes=VMEM_LIMIT),
        name="paste",
    )(boxes, slots, decoded, back, rest)


def solution(mesh):
    return jax.shard_map(
        shards,
        mesh=mesh,
        in_specs=(
            P("sess", "tile", None, None),
            P(),
            P(),
            P(),
            P(),
            P(),
            P(),
            P(None, "sess"),
            P("sess"),
        ),
        out_specs=(P("sess", "tile", None, None), P(("sess", "tile"), None, None, None)),
        check_vma=False,
    )
```

```python
import jax
import jax.numpy as jnp
from jax import lax
from jax.experimental import pallas as pl
from jax.experimental.pallas import tpu as pltpu
from jax.sharding import PartitionSpec as P

S = 64
UNIT = 12
SPAN = 48
C = 128
BANDS = 6
COLS = 320
STRIDE = 64
TILES = 32
CAP = 2
FRAME = BANDS * STRIDE
RIMMED = SPAN + 2
SENT = 104
MESH = pl.DeviceIdType.MESH
BF = jnp.bfloat16
F32 = jnp.float32
CHUNK = 4
U_DEC = 2
U_CONV1 = 2
U_CONV2 = 4
U_PATCH = 8
EARLY = 2
VMEM_LIMIT = 60 * 1024 * 1024

OFFSETS = sorted(
    [(dy, dx, dc) for dy in range(4) for dx in range(4) for dc in range(2) if dy + dx + dc],
    key=lambda d: -(min(d[0], 4 - d[0]) + min(d[1], 4 - d[1])),
)
PEERS = len(OFFSETS)


def silu(v):
    half = 0.5 * v
    return half + half * jnp.tanh(half)


def rounded(v):
    return v.astype(BF).astype(F32)


def pair_weight(w_ref, out_ref):
    zero = jnp.zeros((C, C), BF)
    for a in range(4):
        for dx in range(3):
            rows = pl.ds((a * 3 + dx) * C, C)
            out_ref[rows, 0:C] = w_ref[3 * a + dx] if a < 3 else zero
            out_ref[rows, C : 2 * C] = w_ref[3 * (a - 1) + dx] if a > 0 else zero


def widen(pad_ref, index, start, cols):
    return jnp.concatenate(
        [pad_ref[index, pl.ds(start + dx, cols), :].astype(BF) for dx in range(3)], axis=-1
    )


def spread_row(v):
    cell = lax.broadcasted_iota(jnp.int32, (8, C), 0)
    left = pltpu.roll(v, 1, 0)
    left = jnp.concatenate([jnp.where(cell == 0, 0.0, left[0:8]), left[8:]], axis=0)
    right = pltpu.roll(v, S - 1, 0)
    right = jnp.concatenate([right[: S - 8], jnp.where(cell == 7, 0.0, right[S - 8 :])], axis=0)
    return jnp.concatenate([left.astype(BF), v.astype(BF), right.astype(BF)], axis=-1)


def conv_pairs(wide, w_pair, bias, m0, cols):
    lhs = jnp.concatenate(
        [
            wide[pl.ds(m0 + a // 2, CHUNK), a % 2].reshape(CHUNK * cols, 3 * C)
            for a in range(4)
        ],
        axis=-1,
    )
    return jnp.dot(lhs, w_pair[...], preferred_element_type=F32) + bias


def twice(b_ref):
    return jnp.concatenate([b_ref[...], b_ref[...]], axis=-1)


def main_kernel(
    boxes,
    slots,
    feat_in,
    w0_in,
    b0,
    w1_in,
    b1,
    w2_in,
    b2,
    dec_out,
    rest_out,
    back,
    feat,
    w0,
    w1,
    w2,
    w0_pair,
    w1_pair,
    w2_pair,
    fpad,
    stage,
    payload,
    got,
    reg,
    wide0,
    value,
    cut,
    wide,
    wide2,
    delta,
    rest,
    ret,
    halo,
    hpad,
    dwide,
    dec,
    crop_tap,
    crop_frac,
    back_tap,
    back_one,
    back_two,
    fwd_send,
    fwd_recv,
    ret_send,
    ret_recv,
    halo_send,
    halo_recv,
    local_sem,
    load_sem,
):
    fetches = [
        pltpu.make_async_copy(feat_in.at[b], feat.at[b], load_sem.at[3 + b]) for b in range(BANDS)
    ]
    for fetch in fetches:
        fetch.start()
    me = lax.axis_index("tile")
    y, x, core = me // 8, (me // 2) % 4, me % 2
    targets = [
        ((y + dy) % 4) * 8 + ((x + dx) % 4) * 2 + (core + dc) % 2 for dy, dx, dc in OFFSETS
    ]
    barrier = pltpu.get_barrier_semaphore()
    for t in targets:
        pl.semaphore_signal(barrier, inc=1, device_id={"tile": t}, device_id_type=MESH)

    def remote(src, dst, send, recv, t):
        return pltpu.make_async_remote_copy(
            src_ref=src,
            dst_ref=dst,
            send_sem=send,
            recv_sem=recv,
            device_id={"tile": t},
            device_id_type=MESH,
        )

    def forward(s):
        return [
            remote(
                payload.at[s, t], got.at[s, me], fwd_send.at[s, k], fwd_recv.at[s, k], t
            )
            for k, t in enumerate(targets)
        ]

    def backward(s):
        return [
            remote(ret.at[s, t], back.at[s, me], ret_send.at[s, k], ret_recv.at[s, k], t)
            for k, t in enumerate(targets)
        ]

    def own_forward(s):
        return pltpu.make_async_copy(payload.at[s, me], got.at[s, me], local_sem.at[s])

    def own_backward(s):
        return pltpu.make_async_copy(ret.at[s, me], back.at[s, me], local_sem.at[2 + s])

    def keep_rest(s):
        return pltpu.make_async_copy(rest.at[s], rest_out.at[s], local_sem.at[4 + s])

    def rims(part):
        after, ahead = (me + 1) % TILES, (me + TILES - 1) % TILES
        bands = pl.ds(0, EARLY) if part == 0 else pl.ds(EARLY, BANDS - EARLY)
        return [
            remote(
                feat.at[bands, 1 - side],
                halo.at[side, bands],
                halo_send.at[part, side],
                halo_recv.at[part, side],
                t,
            )
            for side, t in enumerate((after, ahead))
        ]

    loads = [
        pltpu.make_async_copy(src, dst, load_sem.at[k])
        for k, (src, dst) in enumerate(((w0_in, w0), (w1_in, w1), (w2_in, w2)))
    ]
    for load in loads:
        load.start()
    fpad[:, 0:8, :] = jnp.zeros((2 * BANDS, 8, C), F32)
    fpad[:, COLS + 8 : COLS + 16, :] = jnp.zeros((2 * BANDS, 8, C), F32)
    for b in range(BANDS):
        fetches[b].wait()
        for o in range(2):
            fpad[2 * b + o, 8 : COLS + 8, :] = feat[b, o].astype(F32)

    def fill(s, w, spot):
        crop = jnp.maximum(slots[CAP * w + s], 0)
        row0 = boxes[0, crop] - 1
        col0 = boxes[1, crop]
        for i in range(2):
            h = (2 * me + i - row0) & (STRIDE - 1)
            band = jnp.clip((row0 + h) >> 6, 0, BANDS - 1)
            stage[spot, pl.ds(i * RIMMED, 56), :] = fpad[2 * band + i, pl.ds(col0 + 7, 56), :]
        payload[s, w] = stage[spot, 0:SENT].astype(BF)

    ahead = forward(0)
    step = 4
    for k0 in range(0, PEERS + 1, step):
        for k, w in enumerate((targets + [me])[k0 : k0 + step]):
            fill(0, w, k)
        if k0 == step:
            pl.semaphore_wait(barrier, PEERS)
            for copy in rims(0):
                copy.start()
        for copy in ahead[max(k0 - step, 0) : k0]:
            copy.start()
    for copy in ahead[PEERS + 1 - step :]:
        copy.start()
    own_forward(0).start()

    def fill_next(j, _):
        for k in range(4):
            fill(1, 4 * j + k, k)
        return 0

    lax.fori_loop(0, TILES // 4, fill_next, 0)
    for load in loads:
        load.wait()
    pair_weight(w0, w0_pair)
    pair_weight(w1, w1_pair)
    pair_weight(w2, w2_pair)
    for ref in (wide, wide2):
        ref[0, 0] = jnp.zeros((S, 3 * C), BF)
        ref[S // 2, 1] = jnp.zeros((S, 3 * C), BF)
    reg[TILES] = jnp.zeros((SENT, C), F32)
    def taps(k, _):
        crop = jnp.maximum(slots[CAP * me + k // S], 0)
        side = UNIT * (boxes[2, crop] + 2)
        t = k % S
        num = jnp.clip((2 * t + 1) * side - S, 0, (side - 1) * 128)
        crop_tap[k] = num >> 7
        crop_frac[k] = (num & 127).astype(F32) * (1.0 / 128.0)
        h = (t - boxes[0, crop]) & (STRIDE - 1)
        magic = jnp.where(side == 24, 10923, jnp.where(side == 36, 7282, 5462))
        inverse = jnp.where(side == 24, 1.0 / 24, jnp.where(side == 36, 1.0 / 36, 1.0 / 48))
        num = jnp.clip((2 * h + 1) * (S // 2) - (side >> 1), 0, (S - 1) * side)
        one = (num * magic) >> 18
        frac = (num - one * side).astype(F32) * inverse
        live = (h < side).astype(F32)
        back_tap[k] = one
        back_one[k] = live - live * frac
        back_two[k] = live * frac
        return 0

    lax.fori_loop(0, CAP * S, taps, 0, unroll=4)
    hpad[:, 0:8, :] = jnp.zeros((2, 8, C), F32)
    hpad[:, COLS + 8 : COLS + 16, :] = jnp.zeros((2, 8, C), F32)
    bias0, bias1, bias2 = twice(b0), twice(b1), twice(b2)

    def arrived(s):
        own_forward(s).wait()
        for copy in forward(s):
            copy.wait_recv()

    for copy in forward(0):
        copy.wait_send()
    for copy in forward(1):
        copy.start()
    own_forward(1).start()
    for copy in rims(1):
        copy.start()
    arrived(0)

    def restore(s, _):
        slot = slots[CAP * me + s]
        crop = jnp.maximum(slot, 0)
        row0 = boxes[0, crop]
        side = UNIT * (boxes[2, crop] + 2)
        sidef = side.astype(F32)

        def unpack(p, _):
            reg[p] = got[s, p].astype(F32)
            return 0

        lax.fori_loop(0, TILES, unpack, 0, unroll=8)

        def region(h, _):
            for o in range(2):
                row = row0 - 1 + 2 * h + o
                live = (row >= 0) & (row < FRAME)
                index = jnp.where(live, (row & (STRIDE - 1)) >> 1, TILES)
                wide0[h, o] = widen(reg, index, (row & 1) * RIMMED, SPAN)
            return 0

        lax.fori_loop(0, SPAN // 2 + 1, region, 0, unroll=5)

        spot = (lax.broadcasted_iota(jnp.int32, (S, SPAN), 0).astype(F32) + 0.5) * sidef / S
        spot = jnp.clip(spot - 0.5, 0.0, sidef - 1.0)
        cell = lax.broadcasted_iota(jnp.int32, (S, SPAN), 1).astype(F32)
        down = jnp.maximum(0.0, 1.0 - jnp.abs(spot - cell)).astype(BF)

        def decode(j, _):
            m0 = j * CHUNK
            act = silu(conv_pairs(wide0, w0_pair, bias0, m0, SPAN))
            act = act.reshape(CHUNK, SPAN, 2 * C)
            for i in range(CHUNK):
                centre = jnp.concatenate(
                    [wide0[m0 + i, 1, :, C : 2 * C], wide0[m0 + i + 1, 0, :, C : 2 * C]], axis=-1
                )
                value[m0 + i] = (centre.astype(F32) + act[i]).astype(BF)
            return 0

        lax.fori_loop(0, SPAN // 2 // CHUNK, decode, 0, unroll=U_DEC)

        def colcut(m, _):
            z = rounded(jnp.dot(down, value[m], preferred_element_type=F32))
            cut[2 * m] = z[:, 0:C]
            cut[2 * m + 1] = z[:, C : 2 * C]
            return 0

        lax.fori_loop(0, SPAN // 2, colcut, 0, unroll=12)

        def crop_row(t, _):
            first = crop_tap[s * S + t]
            second = jnp.minimum(first + 1, SPAN - 1)
            frac = crop_frac[s * S + t]
            v = (1.0 - frac) * cut[first] + frac * cut[second]
            wide[(t + 1) >> 1, (t + 1) & 1] = spread_row(v)
            return 0

        lax.fori_loop(0, S, crop_row, 0, unroll=8)
        groups = S // (2 * CHUNK)

        def first_conv(j, _):
            v = silu(conv_pairs(wide, w1_pair, bias1, j * CHUNK, S))
            v = v.reshape(CHUNK, S, 2 * C)
            for i in range(CHUNK):
                wide2[j * CHUNK + i, 1] = spread_row(v[i, :, 0:C])
                wide2[j * CHUNK + i + 1, 0] = spread_row(v[i, :, C : 2 * C])
            return 0

        lax.fori_loop(0, groups, first_conv, 0, unroll=U_CONV1)
        keep = slot >= 0

        def second_conv(j, _):
            v = rounded(conv_pairs(wide2, w2_pair, bias2, j * CHUNK, S))
            v = v.reshape(CHUNK, S, 2 * C)
            for i in range(CHUNK):
                for o in range(2):
                    row = 2 * (j * CHUNK + i) + o
                    part = v[i, :, o * C : (o + 1) * C]
                    delta[row] = part
                    rest[s, row] = jnp.where(keep, part, 0.0).astype(BF)
            return 0

        lax.fori_loop(0, groups, second_conv, 0, unroll=U_CONV2)
        keep_rest(s).start()

        where = (lax.broadcasted_iota(jnp.int32, (SPAN, S), 0).astype(F32) + 0.5) * S / sidef
        where = jnp.clip(where - 0.5, 0.0, S - 1.0)
        inside = lax.broadcasted_iota(jnp.int32, (SPAN, S), 0) < side
        grid = lax.broadcasted_iota(jnp.int32, (SPAN, S), 1).astype(F32)
        lift = jnp.where(inside, jnp.maximum(0.0, 1.0 - jnp.abs(where - grid)), 0.0)
        lift_high = lift.astype(BF)
        lift_low = (lift - lift_high.astype(F32)).astype(BF)
        lifts = jnp.concatenate([lift_high, lift_low], axis=0)
        def patch(p):
            halves = []
            for i in range(2):
                k = s * S + 2 * p + i
                one = back_tap[k]
                two = jnp.minimum(one + 1, S - 1)
                halves.append((back_one[k] * delta[one] + back_two[k] * delta[two]).astype(BF))
            rhs = jnp.concatenate(halves, axis=-1)
            z = jnp.dot(lifts, rhs, preferred_element_type=F32)
            z = (z[0:SPAN] + z[SPAN : 2 * SPAN]).astype(BF)
            ret[s, p, 0] = z[:, 0:C]
            ret[s, p, 1] = z[:, C : 2 * C]

        copies = backward(s)
        for k0 in range(0, PEERS + 1, U_PATCH):
            for t in (targets + [me])[k0 : k0 + U_PATCH]:
                patch(t)
            for copy in copies[max(k0 - U_PATCH, 0) : k0]:
                copy.start()
        for copy in copies[PEERS + 1 - U_PATCH :]:
            copy.start()
        own_backward(s).start()

        @pl.when(s == 0)
        def _():
            arrived(1)

        return 0

    lax.fori_loop(0, CAP, restore, 0)

    for part in range(2):
        for copy in rims(part):
            copy.wait_recv()

    def band(b, _):
        up = jnp.where(me == 0, b - 1, b)
        low = jnp.where(me == TILES - 1, b + 1, b)
        up_ok = (up >= 0).astype(F32)
        low_ok = (low < BANDS).astype(F32)
        hpad[0, 8 : COLS + 8, :] = halo[0, jnp.maximum(up, 0)].astype(F32) * up_ok
        hpad[1, 8 : COLS + 8, :] = halo[1, jnp.minimum(low, BANDS - 1)].astype(F32) * low_ok
        dwide[0] = widen(hpad, 0, 7, COLS)
        dwide[1] = widen(fpad, 2 * b, 7, COLS)
        dwide[2] = widen(fpad, 2 * b + 1, 7, COLS)
        dwide[3] = widen(hpad, 1, 7, COLS)
        for part in range(2):
            rows = pl.ds(part * (COLS // 2), COLS // 2)
            lhs = jnp.concatenate([dwide[a, rows, :] for a in range(4)], axis=-1)
            act = silu(jnp.dot(lhs, w0_pair[...], preferred_element_type=F32) + bias0)
            for o in range(2):
                v = feat[b, o, rows, :].astype(F32) + act[:, o * C : (o + 1) * C]
                dec[b, o, rows, :] = v.astype(BF)
        return 0

    lax.fori_loop(0, BANDS, band, 0)
    out = pltpu.make_async_copy(dec, dec_out, local_sem.at[6])
    out.start()
    for part in range(2):
        for copy in rims(part):
            copy.wait_send()
    for copy in forward(1):
        copy.wait_send()
    for s in range(CAP):
        keep_rest(s).wait()
        own_backward(s).wait()
    for s in range(CAP):
        for copy in backward(s):
            copy.wait()
    out.wait()


def paste_kernel(
    boxes, slots, dec_in, back_in, rest_in, out, rest_out, dec, back, rest, acc, done, sem
):
    position = lax.axis_index("tile")
    fetch_dec = [
        pltpu.make_async_copy(dec_in.at[b], dec.at[b], sem.at[5 + BANDS + b]) for b in range(BANDS)
    ]
    fetch_back = [
        pltpu.make_async_copy(back_in.at[s], back.at[s], sem.at[1 + s]) for s in range(CAP)
    ]
    fetch_rest = pltpu.make_async_copy(rest_in, rest, sem.at[3])
    store_rest = pltpu.make_async_copy(rest, rest_out, sem.at[4])
    for copy in fetch_dec + fetch_back:
        copy.start()
    fetch_rest.start()
    for b in range(BANDS):
        fetch_dec[b].wait()
        for o in range(2):
            acc[2 * b + o] = dec[b, o].astype(F32)

    for s in range(CAP):
        fetch_back[s].wait()

        def body(w, _):
            slot = slots[CAP * w + s]

            @pl.when(slot >= 0)
            def _():
                row0 = boxes[0, slot]
                cols = pl.ds(boxes[1, slot], SPAN)
                rows, sums = [], []
                for i in range(2):
                    h = (2 * position + i - row0) & (STRIDE - 1)
                    rows.append(jnp.where(h < SPAN, 2 * ((row0 + h) >> 6) + i, 2 * BANDS + i))
                    sums.append(acc[rows[i], cols, :] + back[s, w, i].astype(F32))
                for i in range(2):
                    acc[rows[i], cols, :] = sums[i]

            return 0

        lax.fori_loop(0, TILES, body, 0)
        if s == 0:
            fetch_rest.wait()
            store_rest.start()
    stores = []
    for b in range(BANDS):
        for o in range(2):
            done[b, o] = acc[2 * b + o].astype(BF)
        stores.append(pltpu.make_async_copy(done.at[b], out.at[b], sem.at[5 + b]))
        stores[-1].start()
    store_rest.wait()
    for copy in stores:
        copy.wait()


def shards(
    features,
    dec_weight,
    dec_bias,
    first_weight,
    first_bias,
    second_weight,
    second_bias,
    boxes,
    slots,
):
    smem = pl.BlockSpec(memory_space=pltpu.SMEM)
    vmem = pl.BlockSpec(memory_space=pltpu.VMEM)
    any_ = pl.BlockSpec(memory_space=pl.ANY)
    rest_type = jax.ShapeDtypeStruct((CAP, S, S, C), BF)
    frame_type = jax.ShapeDtypeStruct(features.shape, BF)
    dma = pltpu.SemaphoreType.DMA
    pair = pltpu.VMEM((12 * C, 2 * C), BF)
    spread = pltpu.VMEM((S // 2 + 1, 2, S, 3 * C), BF)
    table = (CAP * S,)
    sent = pltpu.VMEM((CAP, TILES, SENT, C), BF)
    weight = pltpu.VMEM((9, C, C), BF)

    decoded, rest, back = pl.pallas_call(
        main_kernel,
        out_shape=(
            frame_type,
            rest_type,
            jax.ShapeDtypeStruct((CAP, TILES, 2, SPAN, C), BF),
        ),
        in_specs=[smem, smem, any_] + [any_, vmem] * 3,
        out_specs=(any_, any_, any_),
        scratch_shapes=[
            pltpu.VMEM((BANDS, 2, COLS, C), BF),
            weight,
            weight,
            weight,
            pair,
            pair,
            pair,
            pltpu.VMEM((2 * BANDS, COLS + 16, C), F32),
            pltpu.VMEM((4, SENT + 8, C), F32),
            sent,
            sent,
            pltpu.VMEM((TILES + 1, SENT, C), F32),
            pltpu.VMEM((SPAN // 2 + 1, 2, SPAN, 3 * C), BF),
            pltpu.VMEM((SPAN // 2, SPAN, 2 * C), BF),
            pltpu.VMEM((SPAN, S, C), F32),
            spread,
            spread,
            pltpu.VMEM((S, S, C), F32),
            pltpu.VMEM((CAP, S, S, C), BF),
            pltpu.VMEM((CAP, TILES, 2, SPAN, C), BF),
            pltpu.VMEM((2, BANDS, COLS, C), BF),
            pltpu.VMEM((2, COLS + 16, C), F32),
            pltpu.VMEM((4, COLS, 3 * C), BF),
            pltpu.VMEM((BANDS, 2, COLS, C), BF),
            pltpu.SMEM(table, jnp.int32),
            pltpu.SMEM(table, F32),
            pltpu.SMEM(table, jnp.int32),
            pltpu.SMEM(table, F32),
            pltpu.SMEM(table, F32),
            dma((CAP, PEERS)),
            dma((CAP, PEERS)),
            dma((CAP, PEERS)),
            dma((CAP, PEERS)),
            dma((2, 2)),
            dma((2, 2)),
            dma((7,)),
            dma((3 + BANDS,)),
        ],
        compiler_params=pltpu.CompilerParams(
            collective_id=0, has_side_effects=True, vmem_limit_bytes=VMEM_LIMIT
        ),
        name="main",
    )(
        boxes,
        slots,
        features,
        dec_weight,
        dec_bias[None],
        first_weight,
        first_bias[None],
        second_weight,
        second_bias[None],
    )

    return pl.pallas_call(
        paste_kernel,
        out_shape=(frame_type, rest_type),
        in_specs=[smem, smem, any_, any_, any_],
        out_specs=(any_, any_),
        scratch_shapes=[
            pltpu.VMEM((BANDS, 2, COLS, C), BF),
            pltpu.VMEM((CAP, TILES, 2, SPAN, C), BF),
            pltpu.VMEM((CAP, S, S, C), BF),
            pltpu.VMEM((2 * BANDS + 2, COLS, C), F32),
            pltpu.VMEM((BANDS, 2, COLS, C), BF),
            dma((5 + 2 * BANDS,)),
        ],
        compiler_params=pltpu.CompilerParams(vmem_limit_bytes=VMEM_LIMIT),
        name="paste",
    )(boxes, slots, decoded, back, rest)


def solution(mesh):
    return jax.shard_map(
        shards,
        mesh=mesh,
        in_specs=(
            P("sess", "tile", None, None),
            P(),
            P(),
            P(),
            P(),
            P(),
            P(),
            P(None, "sess"),
            P("sess"),
        ),
        out_specs=(P("sess", "tile", None, None), P(("sess", "tile"), None, None, None)),
        check_vma=False,
    )
```

```python
import jax
import jax.numpy as jnp
from jax import lax
from jax.experimental import pallas as pl
from jax.experimental.pallas import tpu as pltpu
from jax.sharding import PartitionSpec as P

S = 64
UNIT = 12
SPAN = 48
C = 128
BANDS = 6
COLS = 320
STRIDE = 64
TILES = 32
CAP = 2
FRAME = BANDS * STRIDE
RIMMED = SPAN + 2
SENT = 104
MESH = pl.DeviceIdType.MESH
BF = jnp.bfloat16
F32 = jnp.float32
CHUNK = 4
U_DEC = 2
U_CONV1 = 2
U_CONV2 = 4
U_PATCH = 8
EARLY = 1
VMEM_LIMIT = 60 * 1024 * 1024

OFFSETS = sorted(
    [(dy, dx, dc) for dy in range(4) for dx in range(4) for dc in range(2) if dy + dx + dc],
    key=lambda d: -(min(d[0], 4 - d[0]) + min(d[1], 4 - d[1])),
)
PEERS = len(OFFSETS)


def silu(v):
    half = 0.5 * v
    return half + half * jnp.tanh(half)


def rounded(v):
    return v.astype(BF).astype(F32)


def pair_weight(w_ref, out_ref):
    zero = jnp.zeros((C, C), BF)
    for a in range(4):
        for dx in range(3):
            rows = pl.ds((a * 3 + dx) * C, C)
            out_ref[rows, 0:C] = w_ref[3 * a + dx] if a < 3 else zero
            out_ref[rows, C : 2 * C] = w_ref[3 * (a - 1) + dx] if a > 0 else zero


def widen(pad_ref, index, start, cols):
    return jnp.concatenate(
        [pad_ref[index, pl.ds(start + dx, cols), :].astype(BF) for dx in range(3)], axis=-1
    )


def spread_row(v):
    cell = lax.broadcasted_iota(jnp.int32, (8, C), 0)
    left = pltpu.roll(v, 1, 0)
    left = jnp.concatenate([jnp.where(cell == 0, 0.0, left[0:8]), left[8:]], axis=0)
    right = pltpu.roll(v, S - 1, 0)
    right = jnp.concatenate([right[: S - 8], jnp.where(cell == 7, 0.0, right[S - 8 :])], axis=0)
    return jnp.concatenate([left.astype(BF), v.astype(BF), right.astype(BF)], axis=-1)


def conv_pairs(wide, w_pair, bias, m0, cols):
    lhs = jnp.concatenate(
        [
            wide[pl.ds(m0 + a // 2, CHUNK), a % 2].reshape(CHUNK * cols, 3 * C)
            for a in range(4)
        ],
        axis=-1,
    )
    return jnp.dot(lhs, w_pair[...], preferred_element_type=F32) + bias


def twice(b_ref):
    return jnp.concatenate([b_ref[...], b_ref[...]], axis=-1)


def main_kernel(
    boxes,
    slots,
    feat_in,
    w0_in,
    b0,
    w1_in,
    b1,
    w2_in,
    b2,
    dec_out,
    rest_out,
    back,
    feat,
    w0,
    w1,
    w2,
    w0_pair,
    w1_pair,
    w2_pair,
    fpad,
    stage,
    payload,
    got,
    reg,
    wide0,
    value,
    cut,
    wide,
    wide2,
    delta,
    rest,
    ret,
    halo,
    hpad,
    dwide,
    dec,
    crop_tap,
    crop_frac,
    back_tap,
    back_one,
    back_two,
    fwd_send,
    fwd_recv,
    ret_send,
    ret_recv,
    halo_send,
    halo_recv,
    local_sem,
    load_sem,
):
    fetches = [
        pltpu.make_async_copy(feat_in.at[b], feat.at[b], load_sem.at[3 + b]) for b in range(BANDS)
    ]
    for fetch in fetches:
        fetch.start()
    me = lax.axis_index("tile")
    y, x, core = me // 8, (me // 2) % 4, me % 2
    targets = [
        ((y + dy) % 4) * 8 + ((x + dx) % 4) * 2 + (core + dc) % 2 for dy, dx, dc in OFFSETS
    ]
    barrier = pltpu.get_barrier_semaphore()
    for t in targets:
        pl.semaphore_signal(barrier, inc=1, device_id={"tile": t}, device_id_type=MESH)

    def remote(src, dst, send, recv, t):
        return pltpu.make_async_remote_copy(
            src_ref=src,
            dst_ref=dst,
            send_sem=send,
            recv_sem=recv,
            device_id={"tile": t},
            device_id_type=MESH,
        )

    def forward(s):
        return [
            remote(
                payload.at[s, t], got.at[s, me], fwd_send.at[s, k], fwd_recv.at[s, k], t
            )
            for k, t in enumerate(targets)
        ]

    def backward(s):
        return [
            remote(ret.at[s, t], back.at[s, me], ret_send.at[s, k], ret_recv.at[s, k], t)
            for k, t in enumerate(targets)
        ]

    def own_forward(s):
        return pltpu.make_async_copy(payload.at[s, me], got.at[s, me], local_sem.at[s])

    def own_backward(s):
        return pltpu.make_async_copy(ret.at[s, me], back.at[s, me], local_sem.at[2 + s])

    def keep_rest(s):
        return pltpu.make_async_copy(rest.at[s], rest_out.at[s], local_sem.at[4 + s])

    def rims(part):
        after, ahead = (me + 1) % TILES, (me + TILES - 1) % TILES
        bands = pl.ds(0, EARLY) if part == 0 else pl.ds(EARLY, BANDS - EARLY)
        return [
            remote(
                feat.at[bands, 1 - side],
                halo.at[side, bands],
                halo_send.at[part, side],
                halo_recv.at[part, side],
                t,
            )
            for side, t in enumerate((after, ahead))
        ]

    loads = [
        pltpu.make_async_copy(src, dst, load_sem.at[k])
        for k, (src, dst) in enumerate(((w0_in, w0), (w1_in, w1), (w2_in, w2)))
    ]
    for load in loads:
        load.start()
    fpad[:, 0:8, :] = jnp.zeros((2 * BANDS, 8, C), F32)
    fpad[:, COLS + 8 : COLS + 16, :] = jnp.zeros((2 * BANDS, 8, C), F32)
    for b in range(BANDS):
        fetches[b].wait()
        for o in range(2):
            fpad[2 * b + o, 8 : COLS + 8, :] = feat[b, o].astype(F32)

    def fill(s, w, spot):
        crop = jnp.maximum(slots[CAP * w + s], 0)
        row0 = boxes[0, crop] - 1
        col0 = boxes[1, crop]
        for i in range(2):
            h = (2 * me + i - row0) & (STRIDE - 1)
            band = jnp.clip((row0 + h) >> 6, 0, BANDS - 1)
            stage[spot, pl.ds(i * RIMMED, 56), :] = fpad[2 * band + i, pl.ds(col0 + 7, 56), :]
        payload[s, w] = stage[spot, 0:SENT].astype(BF)

    ahead = forward(0)
    step = 4
    for k0 in range(0, PEERS + 1, step):
        for k, w in enumerate((targets + [me])[k0 : k0 + step]):
            fill(0, w, k)
        if k0 == step:
            pl.semaphore_wait(barrier, PEERS)
            for copy in rims(0):
                copy.start()
        for copy in ahead[max(k0 - step, 0) : k0]:
            copy.start()
    for copy in ahead[PEERS + 1 - step :]:
        copy.start()
    own_forward(0).start()

    def fill_next(j, _):
        for k in range(4):
            fill(1, 4 * j + k, k)
        return 0

    lax.fori_loop(0, TILES // 4, fill_next, 0)
    for load in loads:
        load.wait()
    pair_weight(w0, w0_pair)
    pair_weight(w1, w1_pair)
    pair_weight(w2, w2_pair)
    for ref in (wide, wide2):
        ref[0, 0] = jnp.zeros((S, 3 * C), BF)
        ref[S // 2, 1] = jnp.zeros((S, 3 * C), BF)
    reg[TILES] = jnp.zeros((SENT, C), F32)
    def taps(k, _):
        crop = jnp.maximum(slots[CAP * me + k // S], 0)
        side = UNIT * (boxes[2, crop] + 2)
        t = k % S
        num = jnp.clip((2 * t + 1) * side - S, 0, (side - 1) * 128)
        crop_tap[k] = num >> 7
        crop_frac[k] = (num & 127).astype(F32) * (1.0 / 128.0)
        h = (t - boxes[0, crop]) & (STRIDE - 1)
        magic = jnp.where(side == 24, 10923, jnp.where(side == 36, 7282, 5462))
        inverse = jnp.where(side == 24, 1.0 / 24, jnp.where(side == 36, 1.0 / 36, 1.0 / 48))
        num = jnp.clip((2 * h + 1) * (S // 2) - (side >> 1), 0, (S - 1) * side)
        one = (num * magic) >> 18
        frac = (num - one * side).astype(F32) * inverse
        live = (h < side).astype(F32)
        back_tap[k] = one
        back_one[k] = live - live * frac
        back_two[k] = live * frac
        return 0

    lax.fori_loop(0, CAP * S, taps, 0, unroll=4)
    hpad[:, 0:8, :] = jnp.zeros((2, 8, C), F32)
    hpad[:, COLS + 8 : COLS + 16, :] = jnp.zeros((2, 8, C), F32)
    bias0, bias1, bias2 = twice(b0), twice(b1), twice(b2)

    def arrived(s):
        own_forward(s).wait()
        for copy in forward(s):
            copy.wait_recv()

    for copy in forward(0):
        copy.wait_send()
    for copy in forward(1):
        copy.start()
    own_forward(1).start()
    for copy in rims(1):
        copy.start()
    arrived(0)

    def restore(s, _):
        slot = slots[CAP * me + s]
        crop = jnp.maximum(slot, 0)
        row0 = boxes[0, crop]
        side = UNIT * (boxes[2, crop] + 2)
        sidef = side.astype(F32)

        def unpack(p, _):
            reg[p] = got[s, p].astype(F32)
            return 0

        lax.fori_loop(0, TILES, unpack, 0, unroll=8)

        def region(h, _):
            for o in range(2):
                row = row0 - 1 + 2 * h + o
                live = (row >= 0) & (row < FRAME)
                index = jnp.where(live, (row & (STRIDE - 1)) >> 1, TILES)
                wide0[h, o] = widen(reg, index, (row & 1) * RIMMED, SPAN)
            return 0

        lax.fori_loop(0, SPAN // 2 + 1, region, 0, unroll=5)

        spot = (lax.broadcasted_iota(jnp.int32, (S, SPAN), 0).astype(F32) + 0.5) * sidef / S
        spot = jnp.clip(spot - 0.5, 0.0, sidef - 1.0)
        cell = lax.broadcasted_iota(jnp.int32, (S, SPAN), 1).astype(F32)
        down = jnp.maximum(0.0, 1.0 - jnp.abs(spot - cell)).astype(BF)

        def decode(j, _):
            m0 = j * CHUNK
            act = silu(conv_pairs(wide0, w0_pair, bias0, m0, SPAN))
            act = act.reshape(CHUNK, SPAN, 2 * C)
            for i in range(CHUNK):
                centre = jnp.concatenate(
                    [wide0[m0 + i, 1, :, C : 2 * C], wide0[m0 + i + 1, 0, :, C : 2 * C]], axis=-1
                )
                value[m0 + i] = (centre.astype(F32) + act[i]).astype(BF)
            return 0

        lax.fori_loop(0, SPAN // 2 // CHUNK, decode, 0, unroll=U_DEC)

        def colcut(m, _):
            z = rounded(jnp.dot(down, value[m], preferred_element_type=F32))
            cut[2 * m] = z[:, 0:C]
            cut[2 * m + 1] = z[:, C : 2 * C]
            return 0

        lax.fori_loop(0, SPAN // 2, colcut, 0, unroll=12)

        def crop_row(t, _):
            first = crop_tap[s * S + t]
            second = jnp.minimum(first + 1, SPAN - 1)
            frac = crop_frac[s * S + t]
            v = (1.0 - frac) * cut[first] + frac * cut[second]
            wide[(t + 1) >> 1, (t + 1) & 1] = spread_row(v)
            return 0

        lax.fori_loop(0, S, crop_row, 0, unroll=8)
        groups = S // (2 * CHUNK)

        def first_conv(j, _):
            v = silu(conv_pairs(wide, w1_pair, bias1, j * CHUNK, S))
            v = v.reshape(CHUNK, S, 2 * C)
            for i in range(CHUNK):
                wide2[j * CHUNK + i, 1] = spread_row(v[i, :, 0:C])
                wide2[j * CHUNK + i + 1, 0] = spread_row(v[i, :, C : 2 * C])
            return 0

        lax.fori_loop(0, groups, first_conv, 0, unroll=U_CONV1)
        keep = slot >= 0

        def second_conv(j, _):
            v = rounded(conv_pairs(wide2, w2_pair, bias2, j * CHUNK, S))
            v = v.reshape(CHUNK, S, 2 * C)
            for i in range(CHUNK):
                for o in range(2):
                    row = 2 * (j * CHUNK + i) + o
                    part = v[i, :, o * C : (o + 1) * C]
                    delta[row] = part
                    rest[s, row] = jnp.where(keep, part, 0.0).astype(BF)
            return 0

        lax.fori_loop(0, groups, second_conv, 0, unroll=U_CONV2)
        keep_rest(s).start()

        where = (lax.broadcasted_iota(jnp.int32, (SPAN, S), 0).astype(F32) + 0.5) * S / sidef
        where = jnp.clip(where - 0.5, 0.0, S - 1.0)
        inside = lax.broadcasted_iota(jnp.int32, (SPAN, S), 0) < side
        grid = lax.broadcasted_iota(jnp.int32, (SPAN, S), 1).astype(F32)
        lift = jnp.where(inside, jnp.maximum(0.0, 1.0 - jnp.abs(where - grid)), 0.0)
        lift_high = lift.astype(BF)
        lift_low = (lift - lift_high.astype(F32)).astype(BF)
        lifts = jnp.concatenate([lift_high, lift_low], axis=0)
        def patch(p):
            halves = []
            for i in range(2):
                k = s * S + 2 * p + i
                one = back_tap[k]
                two = jnp.minimum(one + 1, S - 1)
                halves.append((back_one[k] * delta[one] + back_two[k] * delta[two]).astype(BF))
            rhs = jnp.concatenate(halves, axis=-1)
            z = jnp.dot(lifts, rhs, preferred_element_type=F32)
            z = (z[0:SPAN] + z[SPAN : 2 * SPAN]).astype(BF)
            ret[s, p, 0] = z[:, 0:C]
            ret[s, p, 1] = z[:, C : 2 * C]

        copies = backward(s)
        for k0 in range(0, PEERS + 1, U_PATCH):
            for t in (targets + [me])[k0 : k0 + U_PATCH]:
                patch(t)
            for copy in copies[max(k0 - U_PATCH, 0) : k0]:
                copy.start()
        for copy in copies[PEERS + 1 - U_PATCH :]:
            copy.start()
        own_backward(s).start()

        @pl.when(s == 0)
        def _():
            arrived(1)

        return 0

    lax.fori_loop(0, CAP, restore, 0)

    for part in range(2):
        for copy in rims(part):
            copy.wait_recv()

    def band(b, _):
        up = jnp.where(me == 0, b - 1, b)
        low = jnp.where(me == TILES - 1, b + 1, b)
        up_ok = (up >= 0).astype(F32)
        low_ok = (low < BANDS).astype(F32)
        hpad[0, 8 : COLS + 8, :] = halo[0, jnp.maximum(up, 0)].astype(F32) * up_ok
        hpad[1, 8 : COLS + 8, :] = halo[1, jnp.minimum(low, BANDS - 1)].astype(F32) * low_ok
        dwide[0] = widen(hpad, 0, 7, COLS)
        dwide[1] = widen(fpad, 2 * b, 7, COLS)
        dwide[2] = widen(fpad, 2 * b + 1, 7, COLS)
        dwide[3] = widen(hpad, 1, 7, COLS)
        for part in range(2):
            rows = pl.ds(part * (COLS // 2), COLS // 2)
            lhs = jnp.concatenate([dwide[a, rows, :] for a in range(4)], axis=-1)
            act = silu(jnp.dot(lhs, w0_pair[...], preferred_element_type=F32) + bias0)
            for o in range(2):
                v = feat[b, o, rows, :].astype(F32) + act[:, o * C : (o + 1) * C]
                dec[b, o, rows, :] = v.astype(BF)
        return 0

    lax.fori_loop(0, BANDS, band, 0)
    out = pltpu.make_async_copy(dec, dec_out, local_sem.at[6])
    out.start()
    for part in range(2):
        for copy in rims(part):
            copy.wait_send()
    for copy in forward(1):
        copy.wait_send()
    for s in range(CAP):
        keep_rest(s).wait()
        own_backward(s).wait()
    for s in range(CAP):
        for copy in backward(s):
            copy.wait()
    out.wait()


def paste_kernel(
    boxes, slots, dec_in, back_in, rest_in, out, rest_out, dec, back, rest, acc, done, sem
):
    position = lax.axis_index("tile")
    fetch_dec = pltpu.make_async_copy(dec_in, dec, sem.at[0])
    fetch_back = [
        pltpu.make_async_copy(back_in.at[s], back.at[s], sem.at[1 + s]) for s in range(CAP)
    ]
    fetch_rest = pltpu.make_async_copy(rest_in, rest, sem.at[3])
    store_rest = pltpu.make_async_copy(rest, rest_out, sem.at[4])
    fetch_dec.start()
    for copy in fetch_back:
        copy.start()
    fetch_rest.start()
    fetch_dec.wait()
    for b in range(BANDS):
        for o in range(2):
            acc[2 * b + o] = dec[b, o].astype(F32)

    for s in range(CAP):
        fetch_back[s].wait()

        def body(w, _):
            slot = slots[CAP * w + s]

            @pl.when(slot >= 0)
            def _():
                row0 = boxes[0, slot]
                cols = pl.ds(boxes[1, slot], SPAN)
                for i in range(2):
                    h = (2 * position + i - row0) & (STRIDE - 1)
                    row = jnp.where(h < SPAN, 2 * ((row0 + h) >> 6) + i, 2 * BANDS + i)
                    acc[row, cols, :] = acc[row, cols, :] + back[s, w, i].astype(F32)

            return 0

        lax.fori_loop(0, TILES, body, 0)
        if s == 0:
            fetch_rest.wait()
            store_rest.start()
    stores = []
    for b in range(BANDS):
        for o in range(2):
            done[b, o] = acc[2 * b + o].astype(BF)
        stores.append(pltpu.make_async_copy(done.at[b], out.at[b], sem.at[5 + b]))
        stores[-1].start()
    store_rest.wait()
    for copy in stores:
        copy.wait()


def shards(
    features,
    dec_weight,
    dec_bias,
    first_weight,
    first_bias,
    second_weight,
    second_bias,
    boxes,
    slots,
):
    smem = pl.BlockSpec(memory_space=pltpu.SMEM)
    vmem = pl.BlockSpec(memory_space=pltpu.VMEM)
    any_ = pl.BlockSpec(memory_space=pl.ANY)
    rest_type = jax.ShapeDtypeStruct((CAP, S, S, C), BF)
    frame_type = jax.ShapeDtypeStruct(features.shape, BF)
    dma = pltpu.SemaphoreType.DMA
    pair = pltpu.VMEM((12 * C, 2 * C), BF)
    spread = pltpu.VMEM((S // 2 + 1, 2, S, 3 * C), BF)
    table = (CAP * S,)
    sent = pltpu.VMEM((CAP, TILES, SENT, C), BF)
    weight = pltpu.VMEM((9, C, C), BF)

    decoded, rest, back = pl.pallas_call(
        main_kernel,
        out_shape=(
            frame_type,
            rest_type,
            jax.ShapeDtypeStruct((CAP, TILES, 2, SPAN, C), BF),
        ),
        in_specs=[smem, smem, any_] + [any_, vmem] * 3,
        out_specs=(any_, any_, any_),
        scratch_shapes=[
            pltpu.VMEM((BANDS, 2, COLS, C), BF),
            weight,
            weight,
            weight,
            pair,
            pair,
            pair,
            pltpu.VMEM((2 * BANDS, COLS + 16, C), F32),
            pltpu.VMEM((4, SENT + 8, C), F32),
            sent,
            sent,
            pltpu.VMEM((TILES + 1, SENT, C), F32),
            pltpu.VMEM((SPAN // 2 + 1, 2, SPAN, 3 * C), BF),
            pltpu.VMEM((SPAN // 2, SPAN, 2 * C), BF),
            pltpu.VMEM((SPAN, S, C), F32),
            spread,
            spread,
            pltpu.VMEM((S, S, C), F32),
            pltpu.VMEM((CAP, S, S, C), BF),
            pltpu.VMEM((CAP, TILES, 2, SPAN, C), BF),
            pltpu.VMEM((2, BANDS, COLS, C), BF),
            pltpu.VMEM((2, COLS + 16, C), F32),
            pltpu.VMEM((4, COLS, 3 * C), BF),
            pltpu.VMEM((BANDS, 2, COLS, C), BF),
            pltpu.SMEM(table, jnp.int32),
            pltpu.SMEM(table, F32),
            pltpu.SMEM(table, jnp.int32),
            pltpu.SMEM(table, F32),
            pltpu.SMEM(table, F32),
            dma((CAP, PEERS)),
            dma((CAP, PEERS)),
            dma((CAP, PEERS)),
            dma((CAP, PEERS)),
            dma((2, 2)),
            dma((2, 2)),
            dma((7,)),
            dma((3 + BANDS,)),
        ],
        compiler_params=pltpu.CompilerParams(
            collective_id=0, has_side_effects=True, vmem_limit_bytes=VMEM_LIMIT
        ),
        name="main",
    )(
        boxes,
        slots,
        features,
        dec_weight,
        dec_bias[None],
        first_weight,
        first_bias[None],
        second_weight,
        second_bias[None],
    )

    return pl.pallas_call(
        paste_kernel,
        out_shape=(frame_type, rest_type),
        in_specs=[smem, smem, any_, any_, any_],
        out_specs=(any_, any_),
        scratch_shapes=[
            pltpu.VMEM((BANDS, 2, COLS, C), BF),
            pltpu.VMEM((CAP, TILES, 2, SPAN, C), BF),
            pltpu.VMEM((CAP, S, S, C), BF),
            pltpu.VMEM((2 * BANDS + 2, COLS, C), F32),
            pltpu.VMEM((BANDS, 2, COLS, C), BF),
            dma((5 + BANDS,)),
        ],
        compiler_params=pltpu.CompilerParams(vmem_limit_bytes=VMEM_LIMIT),
        name="paste",
    )(boxes, slots, decoded, back, rest)


def solution(mesh):
    return jax.shard_map(
        shards,
        mesh=mesh,
        in_specs=(
            P("sess", "tile", None, None),
            P(),
            P(),
            P(),
            P(),
            P(),
            P(),
            P(None, "sess"),
            P("sess"),
        ),
        out_specs=(P("sess", "tile", None, None), P(("sess", "tile"), None, None, None)),
        check_vma=False,
    )
```

```python
import jax
import jax.numpy as jnp
from jax import lax
from jax.experimental import pallas as pl
from jax.experimental.pallas import tpu as pltpu
from jax.sharding import PartitionSpec as P

S = 64
UNIT = 12
SPAN = 48
C = 128
BANDS = 6
COLS = 320
STRIDE = 64
TILES = 32
CAP = 2
FRAME = BANDS * STRIDE
RIMMED = SPAN + 2
SENT = 104
MESH = pl.DeviceIdType.MESH
BF = jnp.bfloat16
F32 = jnp.float32
CHUNK = 4
U_DEC = 2
U_CONV1 = 2
U_CONV2 = 4
U_PATCH = 8
EARLY = 3
VMEM_LIMIT = 60 * 1024 * 1024

OFFSETS = sorted(
    [(dy, dx, dc) for dy in range(4) for dx in range(4) for dc in range(2) if dy + dx + dc],
    key=lambda d: -(min(d[0], 4 - d[0]) + min(d[1], 4 - d[1])),
)
PEERS = len(OFFSETS)


def silu(v):
    half = 0.5 * v
    return half + half * jnp.tanh(half)


def rounded(v):
    return v.astype(BF).astype(F32)


def pair_weight(w_ref, out_ref):
    zero = jnp.zeros((C, C), BF)
    for a in range(4):
        for dx in range(3):
            rows = pl.ds((a * 3 + dx) * C, C)
            out_ref[rows, 0:C] = w_ref[3 * a + dx] if a < 3 else zero
            out_ref[rows, C : 2 * C] = w_ref[3 * (a - 1) + dx] if a > 0 else zero


def widen(pad_ref, index, start, cols):
    return jnp.concatenate(
        [pad_ref[index, pl.ds(start + dx, cols), :].astype(BF) for dx in range(3)], axis=-1
    )


def spread_row(v):
    cell = lax.broadcasted_iota(jnp.int32, (8, C), 0)
    left = pltpu.roll(v, 1, 0)
    left = jnp.concatenate([jnp.where(cell == 0, 0.0, left[0:8]), left[8:]], axis=0)
    right = pltpu.roll(v, S - 1, 0)
    right = jnp.concatenate([right[: S - 8], jnp.where(cell == 7, 0.0, right[S - 8 :])], axis=0)
    return jnp.concatenate([left.astype(BF), v.astype(BF), right.astype(BF)], axis=-1)


def conv_pairs(wide, w_pair, bias, m0, cols):
    lhs = jnp.concatenate(
        [
            wide[pl.ds(m0 + a // 2, CHUNK), a % 2].reshape(CHUNK * cols, 3 * C)
            for a in range(4)
        ],
        axis=-1,
    )
    return jnp.dot(lhs, w_pair[...], preferred_element_type=F32) + bias


def twice(b_ref):
    return jnp.concatenate([b_ref[...], b_ref[...]], axis=-1)


def main_kernel(
    boxes,
    slots,
    feat_in,
    w0_in,
    b0,
    w1_in,
    b1,
    w2_in,
    b2,
    dec_out,
    rest_out,
    back,
    feat,
    w0,
    w1,
    w2,
    w0_pair,
    w1_pair,
    w2_pair,
    fpad,
    stage,
    payload,
    got,
    reg,
    wide0,
    value,
    cut,
    wide,
    wide2,
    delta,
    rest,
    ret,
    halo,
    hpad,
    dwide,
    dec,
    crop_tap,
    crop_frac,
    back_tap,
    back_one,
    back_two,
    fwd_send,
    fwd_recv,
    ret_send,
    ret_recv,
    halo_send,
    halo_recv,
    local_sem,
    load_sem,
):
    fetches = [
        pltpu.make_async_copy(feat_in.at[b], feat.at[b], load_sem.at[3 + b]) for b in range(BANDS)
    ]
    for fetch in fetches:
        fetch.start()
    me = lax.axis_index("tile")
    y, x, core = me // 8, (me // 2) % 4, me % 2
    targets = [
        ((y + dy) % 4) * 8 + ((x + dx) % 4) * 2 + (core + dc) % 2 for dy, dx, dc in OFFSETS
    ]
    barrier = pltpu.get_barrier_semaphore()
    for t in targets:
        pl.semaphore_signal(barrier, inc=1, device_id={"tile": t}, device_id_type=MESH)

    def remote(src, dst, send, recv, t):
        return pltpu.make_async_remote_copy(
            src_ref=src,
            dst_ref=dst,
            send_sem=send,
            recv_sem=recv,
            device_id={"tile": t},
            device_id_type=MESH,
        )

    def forward(s):
        return [
            remote(
                payload.at[s, t], got.at[s, me], fwd_send.at[s, k], fwd_recv.at[s, k], t
            )
            for k, t in enumerate(targets)
        ]

    def backward(s):
        return [
            remote(ret.at[s, t], back.at[s, me], ret_send.at[s, k], ret_recv.at[s, k], t)
            for k, t in enumerate(targets)
        ]

    def own_forward(s):
        return pltpu.make_async_copy(payload.at[s, me], got.at[s, me], local_sem.at[s])

    def own_backward(s):
        return pltpu.make_async_copy(ret.at[s, me], back.at[s, me], local_sem.at[2 + s])

    def keep_rest(s):
        return pltpu.make_async_copy(rest.at[s], rest_out.at[s], local_sem.at[4 + s])

    def rims(part):
        after, ahead = (me + 1) % TILES, (me + TILES - 1) % TILES
        bands = pl.ds(0, EARLY) if part == 0 else pl.ds(EARLY, BANDS - EARLY)
        return [
            remote(
                feat.at[bands, 1 - side],
                halo.at[side, bands],
                halo_send.at[part, side],
                halo_recv.at[part, side],
                t,
            )
            for side, t in enumerate((after, ahead))
        ]

    loads = [
        pltpu.make_async_copy(src, dst, load_sem.at[k])
        for k, (src, dst) in enumerate(((w0_in, w0), (w1_in, w1), (w2_in, w2)))
    ]
    for load in loads:
        load.start()
    fpad[:, 0:8, :] = jnp.zeros((2 * BANDS, 8, C), F32)
    fpad[:, COLS + 8 : COLS + 16, :] = jnp.zeros((2 * BANDS, 8, C), F32)
    for b in range(BANDS):
        fetches[b].wait()
        for o in range(2):
            fpad[2 * b + o, 8 : COLS + 8, :] = feat[b, o].astype(F32)

    def fill(s, w, spot):
        crop = jnp.maximum(slots[CAP * w + s], 0)
        row0 = boxes[0, crop] - 1
        col0 = boxes[1, crop]
        for i in range(2):
            h = (2 * me + i - row0) & (STRIDE - 1)
            band = jnp.clip((row0 + h) >> 6, 0, BANDS - 1)
            stage[spot, pl.ds(i * RIMMED, 56), :] = fpad[2 * band + i, pl.ds(col0 + 7, 56), :]
        payload[s, w] = stage[spot, 0:SENT].astype(BF)

    ahead = forward(0)
    step = 4
    for k0 in range(0, PEERS + 1, step):
        for k, w in enumerate((targets + [me])[k0 : k0 + step]):
            fill(0, w, k)
        if k0 == step:
            pl.semaphore_wait(barrier, PEERS)
            for copy in rims(0):
                copy.start()
        for copy in ahead[max(k0 - step, 0) : k0]:
            copy.start()
    for copy in ahead[PEERS + 1 - step :]:
        copy.start()
    own_forward(0).start()

    def fill_next(j, _):
        for k in range(4):
            fill(1, 4 * j + k, k)
        return 0

    lax.fori_loop(0, TILES // 4, fill_next, 0)
    for load in loads:
        load.wait()
    pair_weight(w0, w0_pair)
    pair_weight(w1, w1_pair)
    pair_weight(w2, w2_pair)
    for ref in (wide, wide2):
        ref[0, 0] = jnp.zeros((S, 3 * C), BF)
        ref[S // 2, 1] = jnp.zeros((S, 3 * C), BF)
    reg[TILES] = jnp.zeros((SENT, C), F32)
    def taps(k, _):
        crop = jnp.maximum(slots[CAP * me + k // S], 0)
        side = UNIT * (boxes[2, crop] + 2)
        t = k % S
        num = jnp.clip((2 * t + 1) * side - S, 0, (side - 1) * 128)
        crop_tap[k] = num >> 7
        crop_frac[k] = (num & 127).astype(F32) * (1.0 / 128.0)
        h = (t - boxes[0, crop]) & (STRIDE - 1)
        magic = jnp.where(side == 24, 10923, jnp.where(side == 36, 7282, 5462))
        inverse = jnp.where(side == 24, 1.0 / 24, jnp.where(side == 36, 1.0 / 36, 1.0 / 48))
        num = jnp.clip((2 * h + 1) * (S // 2) - (side >> 1), 0, (S - 1) * side)
        one = (num * magic) >> 18
        frac = (num - one * side).astype(F32) * inverse
        live = (h < side).astype(F32)
        back_tap[k] = one
        back_one[k] = live - live * frac
        back_two[k] = live * frac
        return 0

    lax.fori_loop(0, CAP * S, taps, 0, unroll=4)
    hpad[:, 0:8, :] = jnp.zeros((2, 8, C), F32)
    hpad[:, COLS + 8 : COLS + 16, :] = jnp.zeros((2, 8, C), F32)
    bias0, bias1, bias2 = twice(b0), twice(b1), twice(b2)

    def arrived(s):
        own_forward(s).wait()
        for copy in forward(s):
            copy.wait_recv()

    for copy in forward(0):
        copy.wait_send()
    for copy in forward(1):
        copy.start()
    own_forward(1).start()
    for copy in rims(1):
        copy.start()
    arrived(0)

    def restore(s, _):
        slot = slots[CAP * me + s]
        crop = jnp.maximum(slot, 0)
        row0 = boxes[0, crop]
        side = UNIT * (boxes[2, crop] + 2)
        sidef = side.astype(F32)

        def unpack(p, _):
            reg[p] = got[s, p].astype(F32)
            return 0

        lax.fori_loop(0, TILES, unpack, 0, unroll=8)

        def region(h, _):
            for o in range(2):
                row = row0 - 1 + 2 * h + o
                live = (row >= 0) & (row < FRAME)
                index = jnp.where(live, (row & (STRIDE - 1)) >> 1, TILES)
                wide0[h, o] = widen(reg, index, (row & 1) * RIMMED, SPAN)
            return 0

        lax.fori_loop(0, SPAN // 2 + 1, region, 0, unroll=5)

        spot = (lax.broadcasted_iota(jnp.int32, (S, SPAN), 0).astype(F32) + 0.5) * sidef / S
        spot = jnp.clip(spot - 0.5, 0.0, sidef - 1.0)
        cell = lax.broadcasted_iota(jnp.int32, (S, SPAN), 1).astype(F32)
        down = jnp.maximum(0.0, 1.0 - jnp.abs(spot - cell)).astype(BF)

        def decode(j, _):
            m0 = j * CHUNK
            act = silu(conv_pairs(wide0, w0_pair, bias0, m0, SPAN))
            act = act.reshape(CHUNK, SPAN, 2 * C)
            for i in range(CHUNK):
                centre = jnp.concatenate(
                    [wide0[m0 + i, 1, :, C : 2 * C], wide0[m0 + i + 1, 0, :, C : 2 * C]], axis=-1
                )
                value[m0 + i] = (centre.astype(F32) + act[i]).astype(BF)
            return 0

        lax.fori_loop(0, SPAN // 2 // CHUNK, decode, 0, unroll=U_DEC)

        def colcut(m, _):
            z = rounded(jnp.dot(down, value[m], preferred_element_type=F32))
            cut[2 * m] = z[:, 0:C]
            cut[2 * m + 1] = z[:, C : 2 * C]
            return 0

        lax.fori_loop(0, SPAN // 2, colcut, 0, unroll=12)

        def crop_row(t, _):
            first = crop_tap[s * S + t]
            second = jnp.minimum(first + 1, SPAN - 1)
            frac = crop_frac[s * S + t]
            v = (1.0 - frac) * cut[first] + frac * cut[second]
            wide[(t + 1) >> 1, (t + 1) & 1] = spread_row(v)
            return 0

        lax.fori_loop(0, S, crop_row, 0, unroll=8)
        groups = S // (2 * CHUNK)

        def first_conv(j, _):
            v = silu(conv_pairs(wide, w1_pair, bias1, j * CHUNK, S))
            v = v.reshape(CHUNK, S, 2 * C)
            for i in range(CHUNK):
                wide2[j * CHUNK + i, 1] = spread_row(v[i, :, 0:C])
                wide2[j * CHUNK + i + 1, 0] = spread_row(v[i, :, C : 2 * C])
            return 0

        lax.fori_loop(0, groups, first_conv, 0, unroll=U_CONV1)
        keep = slot >= 0

        def second_conv(j, _):
            v = rounded(conv_pairs(wide2, w2_pair, bias2, j * CHUNK, S))
            v = v.reshape(CHUNK, S, 2 * C)
            for i in range(CHUNK):
                for o in range(2):
                    row = 2 * (j * CHUNK + i) + o
                    part = v[i, :, o * C : (o + 1) * C]
                    delta[row] = part
                    rest[s, row] = jnp.where(keep, part, 0.0).astype(BF)
            return 0

        lax.fori_loop(0, groups, second_conv, 0, unroll=U_CONV2)
        keep_rest(s).start()

        where = (lax.broadcasted_iota(jnp.int32, (SPAN, S), 0).astype(F32) + 0.5) * S / sidef
        where = jnp.clip(where - 0.5, 0.0, S - 1.0)
        inside = lax.broadcasted_iota(jnp.int32, (SPAN, S), 0) < side
        grid = lax.broadcasted_iota(jnp.int32, (SPAN, S), 1).astype(F32)
        lift = jnp.where(inside, jnp.maximum(0.0, 1.0 - jnp.abs(where - grid)), 0.0)
        lift_high = lift.astype(BF)
        lift_low = (lift - lift_high.astype(F32)).astype(BF)
        lifts = jnp.concatenate([lift_high, lift_low], axis=0)
        def patch(p):
            halves = []
            for i in range(2):
                k = s * S + 2 * p + i
                one = back_tap[k]
                two = jnp.minimum(one + 1, S - 1)
                halves.append((back_one[k] * delta[one] + back_two[k] * delta[two]).astype(BF))
            rhs = jnp.concatenate(halves, axis=-1)
            z = jnp.dot(lifts, rhs, preferred_element_type=F32)
            z = (z[0:SPAN] + z[SPAN : 2 * SPAN]).astype(BF)
            ret[s, p, 0] = z[:, 0:C]
            ret[s, p, 1] = z[:, C : 2 * C]

        copies = backward(s)
        for k0 in range(0, PEERS + 1, U_PATCH):
            for t in (targets + [me])[k0 : k0 + U_PATCH]:
                patch(t)
            for copy in copies[max(k0 - U_PATCH, 0) : k0]:
                copy.start()
        for copy in copies[PEERS + 1 - U_PATCH :]:
            copy.start()
        own_backward(s).start()

        @pl.when(s == 0)
        def _():
            arrived(1)

        return 0

    lax.fori_loop(0, CAP, restore, 0)

    for part in range(2):
        for copy in rims(part):
            copy.wait_recv()

    def band(b, _):
        up = jnp.where(me == 0, b - 1, b)
        low = jnp.where(me == TILES - 1, b + 1, b)
        up_ok = (up >= 0).astype(F32)
        low_ok = (low < BANDS).astype(F32)
        hpad[0, 8 : COLS + 8, :] = halo[0, jnp.maximum(up, 0)].astype(F32) * up_ok
        hpad[1, 8 : COLS + 8, :] = halo[1, jnp.minimum(low, BANDS - 1)].astype(F32) * low_ok
        dwide[0] = widen(hpad, 0, 7, COLS)
        dwide[1] = widen(fpad, 2 * b, 7, COLS)
        dwide[2] = widen(fpad, 2 * b + 1, 7, COLS)
        dwide[3] = widen(hpad, 1, 7, COLS)
        for part in range(2):
            rows = pl.ds(part * (COLS // 2), COLS // 2)
            lhs = jnp.concatenate([dwide[a, rows, :] for a in range(4)], axis=-1)
            act = silu(jnp.dot(lhs, w0_pair[...], preferred_element_type=F32) + bias0)
            for o in range(2):
                v = feat[b, o, rows, :].astype(F32) + act[:, o * C : (o + 1) * C]
                dec[b, o, rows, :] = v.astype(BF)
        return 0

    lax.fori_loop(0, BANDS, band, 0)
    out = pltpu.make_async_copy(dec, dec_out, local_sem.at[6])
    out.start()
    for part in range(2):
        for copy in rims(part):
            copy.wait_send()
    for copy in forward(1):
        copy.wait_send()
    for s in range(CAP):
        keep_rest(s).wait()
        own_backward(s).wait()
    for s in range(CAP):
        for copy in backward(s):
            copy.wait()
    out.wait()


def paste_kernel(
    boxes, slots, dec_in, back_in, rest_in, out, rest_out, dec, back, rest, acc, done, sem
):
    position = lax.axis_index("tile")
    fetch_dec = pltpu.make_async_copy(dec_in, dec, sem.at[0])
    fetch_back = [
        pltpu.make_async_copy(back_in.at[s], back.at[s], sem.at[1 + s]) for s in range(CAP)
    ]
    fetch_rest = pltpu.make_async_copy(rest_in, rest, sem.at[3])
    store_rest = pltpu.make_async_copy(rest, rest_out, sem.at[4])
    fetch_dec.start()
    for copy in fetch_back:
        copy.start()
    fetch_rest.start()
    fetch_dec.wait()
    for b in range(BANDS):
        for o in range(2):
            acc[2 * b + o] = dec[b, o].astype(F32)

    for s in range(CAP):
        fetch_back[s].wait()

        def body(w, _):
            slot = slots[CAP * w + s]

            @pl.when(slot >= 0)
            def _():
                row0 = boxes[0, slot]
                cols = pl.ds(boxes[1, slot], SPAN)
                for i in range(2):
                    h = (2 * position + i - row0) & (STRIDE - 1)
                    row = jnp.where(h < SPAN, 2 * ((row0 + h) >> 6) + i, 2 * BANDS + i)
                    acc[row, cols, :] = acc[row, cols, :] + back[s, w, i].astype(F32)

            return 0

        lax.fori_loop(0, TILES, body, 0)
        if s == 0:
            fetch_rest.wait()
            store_rest.start()
    stores = []
    for b in range(BANDS):
        for o in range(2):
            done[b, o] = acc[2 * b + o].astype(BF)
        stores.append(pltpu.make_async_copy(done.at[b], out.at[b], sem.at[5 + b]))
        stores[-1].start()
    store_rest.wait()
    for copy in stores:
        copy.wait()


def shards(
    features,
    dec_weight,
    dec_bias,
    first_weight,
    first_bias,
    second_weight,
    second_bias,
    boxes,
    slots,
):
    smem = pl.BlockSpec(memory_space=pltpu.SMEM)
    vmem = pl.BlockSpec(memory_space=pltpu.VMEM)
    any_ = pl.BlockSpec(memory_space=pl.ANY)
    rest_type = jax.ShapeDtypeStruct((CAP, S, S, C), BF)
    frame_type = jax.ShapeDtypeStruct(features.shape, BF)
    dma = pltpu.SemaphoreType.DMA
    pair = pltpu.VMEM((12 * C, 2 * C), BF)
    spread = pltpu.VMEM((S // 2 + 1, 2, S, 3 * C), BF)
    table = (CAP * S,)
    sent = pltpu.VMEM((CAP, TILES, SENT, C), BF)
    weight = pltpu.VMEM((9, C, C), BF)

    decoded, rest, back = pl.pallas_call(
        main_kernel,
        out_shape=(
            frame_type,
            rest_type,
            jax.ShapeDtypeStruct((CAP, TILES, 2, SPAN, C), BF),
        ),
        in_specs=[smem, smem, any_] + [any_, vmem] * 3,
        out_specs=(any_, any_, any_),
        scratch_shapes=[
            pltpu.VMEM((BANDS, 2, COLS, C), BF),
            weight,
            weight,
            weight,
            pair,
            pair,
            pair,
            pltpu.VMEM((2 * BANDS, COLS + 16, C), F32),
            pltpu.VMEM((4, SENT + 8, C), F32),
            sent,
            sent,
            pltpu.VMEM((TILES + 1, SENT, C), F32),
            pltpu.VMEM((SPAN // 2 + 1, 2, SPAN, 3 * C), BF),
            pltpu.VMEM((SPAN // 2, SPAN, 2 * C), BF),
            pltpu.VMEM((SPAN, S, C), F32),
            spread,
            spread,
            pltpu.VMEM((S, S, C), F32),
            pltpu.VMEM((CAP, S, S, C), BF),
            pltpu.VMEM((CAP, TILES, 2, SPAN, C), BF),
            pltpu.VMEM((2, BANDS, COLS, C), BF),
            pltpu.VMEM((2, COLS + 16, C), F32),
            pltpu.VMEM((4, COLS, 3 * C), BF),
            pltpu.VMEM((BANDS, 2, COLS, C), BF),
            pltpu.SMEM(table, jnp.int32),
            pltpu.SMEM(table, F32),
            pltpu.SMEM(table, jnp.int32),
            pltpu.SMEM(table, F32),
            pltpu.SMEM(table, F32),
            dma((CAP, PEERS)),
            dma((CAP, PEERS)),
            dma((CAP, PEERS)),
            dma((CAP, PEERS)),
            dma((2, 2)),
            dma((2, 2)),
            dma((7,)),
            dma((3 + BANDS,)),
        ],
        compiler_params=pltpu.CompilerParams(
            collective_id=0, has_side_effects=True, vmem_limit_bytes=VMEM_LIMIT
        ),
        name="main",
    )(
        boxes,
        slots,
        features,
        dec_weight,
        dec_bias[None],
        first_weight,
        first_bias[None],
        second_weight,
        second_bias[None],
    )

    return pl.pallas_call(
        paste_kernel,
        out_shape=(frame_type, rest_type),
        in_specs=[smem, smem, any_, any_, any_],
        out_specs=(any_, any_),
        scratch_shapes=[
            pltpu.VMEM((BANDS, 2, COLS, C), BF),
            pltpu.VMEM((CAP, TILES, 2, SPAN, C), BF),
            pltpu.VMEM((CAP, S, S, C), BF),
            pltpu.VMEM((2 * BANDS + 2, COLS, C), F32),
            pltpu.VMEM((BANDS, 2, COLS, C), BF),
            dma((5 + BANDS,)),
        ],
        compiler_params=pltpu.CompilerParams(vmem_limit_bytes=VMEM_LIMIT),
        name="paste",
    )(boxes, slots, decoded, back, rest)


def solution(mesh):
    return jax.shard_map(
        shards,
        mesh=mesh,
        in_specs=(
            P("sess", "tile", None, None),
            P(),
            P(),
            P(),
            P(),
            P(),
            P(),
            P(None, "sess"),
            P("sess"),
        ),
        out_specs=(P("sess", "tile", None, None), P(("sess", "tile"), None, None, None)),
        check_vma=False,
    )
```
